512 devices in a mesh: dom: 64 (over z, y), col: 8 (over x, core).
Axes of the slice: x: 4, y: 8, z: 8, core: 2. Of those that a mesh axis runs over, the one named last changes fastest.
Arguments:
- block: float32 [256, 65536], P('col', 'dom'), may hold values from -6 to 6
- basis: float32 [2048, 65536], P('col', 'dom'), may hold values from -0.03125 to 0.03125
- g_tiles: float32 [512, 3, 128, 128], P('dom'), may hold values from -24 to 24
- c_tiles: float32 [512, 3, 128, 128], P('dom'), may hold values from -24 to 24
- tile_cols: int32 [512, 3], P('dom'), may hold values from 0 to 9, as said below
- bnd_rows: int32 [8192], P('dom'), may hold values from 0 to 1023, as said below
- dinv: float32 [65536], P('dom'), may hold values from 0.004 to 0.04
- port_nodes: int32 [256], replicated, may hold values from 0 to 65535, as said below
Outputs:
- new_block: float32 [256, 65536], P('col', 'dom')
- coeffs: float32 [2048, 256], P('col')
- chol_factor: float32 [256, 256], P('col')
- port_proj: float32 [2048, 256], P('col')
- g_proj: float32 [2048, 256], P('col')
- c_proj: float32 [2048, 256], P('col')
- g_new: float32 [256, 256], P('col')
- c_new: float32 [256, 256], P('col')
The draws below stay inside these ranges and needn't reach their ends.
Inputs may be any that keep to these rules, and one draw needn't show every extreme that they name: `tile_cols`: entry 0 of row tile r of a partition is r itself; entry 1 of its row tile 0 is 8 and entry 2 of its last row tile is 9. `bnd_rows`: each partition's 128 entries are distinct. `port_nodes`: distinct nodes.
All inputs are finite; a program needn't handle non-finite values.
Results may differ from the reference program's by a relative error of at most 0.00015.
Values sent between devices are 32-bit elements; how exact they have to be, the bound alone decides.
No kernel may reach another device: no remote copies, remote signals or barrier semaphores. Data moves between devices by JAX's collectives and lax.ppermute only.
A program may use at most 64 MiB of HBM per device.

```python
import math
import jax
import jax.numpy as jnp
from jax import lax

TILE = 128
NBRS = 3
PORTS = 256
BASIS = 2048
ROWS_DEV = 1024
TILES_DEV = 8
PARTITIONS = 64
NODES = 65536
ROW_TILES = 512
EDGES = 8192


mixing_share = 0.5


def distinct_with_ends(key, span, count):
    key_one = jax.random.fold_in(key, 11)
    key_two = jax.random.fold_in(key, 12)
    middle = jax.random.permutation(key_one, span - 2)[:count - 2].astype(jnp.int32) + 1
    chosen = jnp.concatenate([jnp.zeros((1,), jnp.int32), middle, jnp.full((1,), span - 1, jnp.int32)])
    order = jax.random.permutation(key_two, count).astype(jnp.int32)
    return chosen[order]


def draw_basis(key, part):
    key_noise = jax.random.fold_in(key, 21)
    key_phase = jax.random.fold_in(key, 22)
    noise = jax.random.truncated_normal(key_noise, -4.0, 4.0, (BASIS, NODES), jnp.float32)
    partner = jnp.roll(noise, BASIS // 2, axis=0)
    mixed = (noise + mixing_share * partner) / math.sqrt(1.0 + mixing_share * mixing_share)
    phase = jax.random.randint(key_phase, (), 0, 4).astype(jnp.int32)
    position = (jnp.arange(NODES, dtype=jnp.int32) + phase) % 4
    node_gain = jnp.where(position == 0, 1.35, jnp.where(position == 1, 0.65, 1.0)).astype(jnp.float32)
    node_gain = node_gain / math.sqrt(1.06125)
    return (mixed * node_gain[None, :] * NODES ** (-0.5)).astype(jnp.float32)


def draw_tile_cols(key, part):
    random_cols = jax.random.randint(jax.random.fold_in(key, 3), (ROW_TILES, NBRS), 0, TILES_DEV + 2).astype(jnp.int32)
    local_tile = (jnp.arange(ROW_TILES, dtype=jnp.int32) % TILES_DEV).astype(jnp.int32)
    random_cols = random_cols.at[:, 0].set(local_tile)
    random_cols = random_cols.at[:, 1].set(jnp.where(local_tile == 0, TILES_DEV, random_cols[:, 1]).astype(jnp.int32))
    random_cols = random_cols.at[:, 2].set(jnp.where(local_tile == TILES_DEV - 1, TILES_DEV + 1, random_cols[:, 2]).astype(jnp.int32))
    return random_cols


def draw_bnd_rows(key, part):
    keys = jax.random.split(jax.random.fold_in(key, 5), PARTITIONS)
    rows_all = jax.vmap(lambda one_key: distinct_with_ends(one_key, ROWS_DEV, TILE))(keys)
    return rows_all.reshape(EDGES).astype(jnp.int32)


def draw_port_nodes(key, part):
    return distinct_with_ends(jax.random.fold_in(key, 7), NODES, PORTS)


def shard_levels(key, extent, shards, smallest, high):
    factor_of = 1.0
    for dim, shards_of in shards:
        draws = jax.random.uniform(jax.random.fold_in(jax.random.fold_in(key, 6), dim), (shards_of,), jnp.float32, smallest / len(shards), high / len(shards))
        factor_of = factor_of * jnp.repeat(jnp.exp(draws), extent[dim] // shards_of).reshape((-1,) + (1,) * (len(extent) - 1 - dim))
    return factor_of


def normal_values(stream_key, extent, width, bound, shards=(), kind=jnp.bfloat16):
    values = jax.random.normal(stream_key, extent, jnp.float32) * width
    if len(shards) > 0:
        values = shard_levels(stream_key, extent, shards, -0.22, 0.18) * values
    return jnp.clip(values, min=-bound, max=bound).astype(kind)


def setup_inputs(seed: int = 0) -> dict:
    seeds = jax.random.split(jax.random.key(seed), 9)
    block = normal_values(seeds[0], (PORTS, NODES), 1.0, 6.0, ((0, 8), (1, 64)), jnp.float32)
    basis = draw_basis(jax.random.fold_in(seeds[8], 71), 0)
    g_tiles = normal_values(seeds[2], (ROW_TILES, NBRS, TILE, TILE), 4.0, 24.0, ((0, 64),), jnp.float32)
    c_tiles = normal_values(seeds[3], (ROW_TILES, NBRS, TILE, TILE), 4.0, 24.0, ((0, 64),), jnp.float32)
    tile_cols = draw_tile_cols(jax.random.fold_in(seeds[8], 71), 0)
    bnd_rows = draw_bnd_rows(jax.random.fold_in(seeds[8], 71), 0)
    dinv = jnp.clip(jnp.exp(math.log(0.04) - 2.30258502 * jax.random.uniform(seeds[6], (NODES,), jnp.float32) ** shard_levels(seeds[6], (NODES,), ((0, 64),), -0.2, 0.2)), 0.004, 0.04)
    port_nodes = draw_port_nodes(jax.random.fold_in(seeds[8], 71), 0)
    return {"block": block, "basis": basis, "g_tiles": g_tiles, "c_tiles": c_tiles, "tile_cols": tile_cols, "bnd_rows": bnd_rows, "dinv": dinv, "port_nodes": port_nodes}


def apply_tiles(tiles, tile_cols, bnd_rows, source):
    count = source.shape[0]
    local_part = source.reshape(count, PARTITIONS, ROWS_DEV).transpose(1, 0, 2)
    edge_idx = bnd_rows.reshape(PARTITIONS, TILE)
    edges = jax.vmap(lambda part_rows, index_rows: part_rows[:, index_rows])(local_part, edge_idx)
    zero_edge = jnp.zeros((1, count, TILE), source.dtype)
    before = jnp.concatenate([zero_edge, edges[:-1]], axis=0)
    after = jnp.concatenate([edges[1:], zero_edge], axis=0)
    extended = jnp.concatenate([local_part, before, after], axis=2)
    tiles_part = tiles.reshape(PARTITIONS, TILES_DEV, NBRS, TILE, TILE)
    cols_part = tile_cols.reshape(PARTITIONS, TILES_DEV, NBRS)

    def one_part(items):
        ext_rows, part_tiles, part_cols = items
        picked = ext_rows.reshape(count, TILES_DEV + 2, TILE)[:, part_cols, :]
        result = jnp.einsum('crkb,rkab->cra', picked, part_tiles, precision=lax.Precision.HIGHEST)
        return result.reshape(count, ROWS_DEV)
    result_all = lax.map(one_part, (extended, tiles_part, cols_part))
    return result_all.transpose(1, 0, 2).reshape(count, NODES)

def inner_rows(left_rows, right_rows):
    return lax.dot_general(left_rows, right_rows, (((1,), (1,)), ((), ())), precision=lax.Precision.HIGHEST)

def remove_part(coeff_rows, basis, source):
    return source - lax.dot_general(coeff_rows, basis, (((0,), (0,)), ((), ())), precision=lax.Precision.HIGHEST)

def reference(block, basis, g_tiles, c_tiles, tile_cols, bnd_rows, dinv, port_nodes):
    work = dinv[None, :] * apply_tiles(c_tiles, tile_cols, bnd_rows, block)
    first_coeff = inner_rows(basis, work)
    first = remove_part(first_coeff, basis, work)
    port_proj = basis[:, port_nodes]
    second_coeff = inner_rows(basis, first)
    second = remove_part(second_coeff, basis, first)
    coeffs = first_coeff + second_coeff
    gram_matrix = inner_rows(second, second)
    chol_factor = jnp.linalg.cholesky(gram_matrix)
    identity = jnp.eye(chol_factor.shape[0], dtype=chol_factor.dtype)
    inverse = jax.scipy.linalg.solve_triangular(chol_factor, identity, lower=True)
    new_block = jnp.dot(inverse, second, precision=lax.Precision.HIGHEST)
    g_image = apply_tiles(g_tiles, tile_cols, bnd_rows, new_block)
    c_image = apply_tiles(c_tiles, tile_cols, bnd_rows, new_block)
    g_proj = inner_rows(basis, g_image)
    c_proj = inner_rows(basis, c_image)
    g_new = inner_rows(new_block, g_image)
    c_new = inner_rows(new_block, c_image)
    return (new_block, coeffs, chol_factor, port_proj, g_proj, c_proj, g_new, c_new)
```

```python
import jax
import jax.numpy as jnp
from jax import lax
from jax.sharding import Mesh
from jax.sharding import PartitionSpec as P

HI = lax.Precision.HIGHEST
DOM = ("z", "y")


def contract(left, right, left_dim, right_dim):
    return lax.dot_general(
        left, right, (((left_dim,), (right_dim,)), ((), ())), precision=HI
    )


def shift(value, axis, step):
    size = lax.axis_size(axis)
    return lax.ppermute(value, axis, [(i, (i + step) % size) for i in range(size)])


def shift_open(value, axis, step):
    size = lax.axis_size(axis)
    pairs = [(i, i + step) for i in range(size) if 0 <= i + step < size]
    return lax.ppermute(value, axis, pairs)


def scatter_sum(pieces, axis):
    return jnp.sum(lax.all_to_all(pieces, axis, 0, 0, tiled=True), axis=0)


def spread(piece, axis):
    size = lax.axis_size(axis)
    copies = jnp.broadcast_to(piece[None], (size,) + piece.shape)
    return lax.all_to_all(copies, axis, 0, 0, tiled=True)


def sum_rows_to_piece(value):
    ny, nz = lax.axis_size("y"), lax.axis_size("z")
    rows, lanes = value.shape
    part = scatter_sum(value.reshape(ny, rows // ny, lanes), "y")
    return scatter_sum(part.reshape(nz, rows // (ny * nz), lanes), "z")


def piece_to_rows(piece):
    rows, lanes = piece.shape
    part = spread(piece, "z").reshape(-1, lanes)
    return spread(part, "y").reshape(-1, lanes)


def sum_dom(value):
    ny, nz = lax.axis_size("y"), lax.axis_size("z")
    rows, lanes = value.shape
    own = rows // ny
    part = scatter_sum(value.reshape(ny, own, lanes), "y")
    piece = scatter_sum(part.reshape(own, nz, lanes // nz).transpose(1, 0, 2), "z")
    part = spread(piece, "z").transpose(1, 0, 2).reshape(own, lanes)
    return spread(part, "y").reshape(rows, lanes)


def dense_tiles(tiles, tile_cols, width):
    count, nbrs, rows, cols = tiles.shape
    hit = tile_cols[:, :, None] == jnp.arange(width, dtype=jnp.int32)
    total = 0.0
    for k in range(nbrs):
        total = total + jnp.where(
            hit[:, k, None, :, None], tiles[:, k, :, None, :], 0.0
        )
    return total.reshape(count * rows, width * cols)


def on_device(block, basis, g_tiles, c_tiles, tile_cols, bnd_rows, dinv, port_nodes):
    tile = g_tiles.shape[-1]
    nodes = block.shape[1]
    own = block.shape[0]
    brows = basis.shape[0]
    width = nodes // tile + 2
    nx = lax.axis_size("x")
    xi = lax.axis_index("x")
    core = lax.axis_index("core")
    dom = lax.axis_index(DOM)
    col = xi * 2 + core
    half = brows // 2

    right = shift(basis, "x", -1)
    left = shift(basis, "x", 1)
    far_low = shift(left[:half], "x", 1)
    far_high = shift(right[half:], "x", -1)
    wide = jnp.concatenate([basis, right, far_low, far_high, left], axis=0)

    node_ids = jnp.arange(nodes, dtype=jnp.int32)
    edge_hot = (bnd_rows[:, None] == node_ids[None, :]).astype(jnp.float32)
    port_hot = ((port_nodes - dom * nodes)[:, None] == node_ids[None, :]).astype(
        jnp.float32
    )

    rim = contract(block, edge_hot, 1, 1)
    before = shift_open(rim, DOM, 1)
    after = shift_open(rim, DOM, -1)
    g_dense = dense_tiles(g_tiles, tile_cols, width)
    c_dense = dense_tiles(c_tiles, tile_cols, width)
    extended = jnp.concatenate([block, before, after], axis=1)
    work = dinv[None, :] * contract(extended, c_dense, 1, 1)
    other = shift(work, "core", 1)
    low = jnp.where(core == 0, work, other)
    high = jnp.where(core == 0, other, work)
    work_chip = jnp.concatenate([low, high], axis=0)

    def transposed(rows):
        outs = []
        for dense in (g_dense, c_dense):
            full = contract(rows, dense, 1, 0)
            back = shift_open(full[:, nodes : nodes + tile], DOM, -1)
            ahead = shift_open(full[:, nodes + tile :], DOM, 1)
            outs.append((full[:, :nodes], back, ahead))
        return outs

    def finish(parts):
        local, back, ahead = parts
        return local + contract(back + ahead, edge_hot, 1, 0)

    basis_parts = transposed(basis)
    port_piece = sum_rows_to_piece(contract(port_hot, basis, 1, 1))
    port_proj = piece_to_rows(port_piece).T
    basis_g, basis_c = [finish(p) for p in basis_parts]

    work_chip, port_proj, basis_g, basis_c = lax.optimization_barrier(
        (work_chip, port_proj, basis_g, basis_c)
    )

    first_coeff = sum_dom(contract(work_chip, wide, 1, 1))
    drop = contract(first_coeff, wide, 1, 0)
    first_chip = work_chip - (drop + shift(drop, "core", 1))
    second_coeff = sum_dom(contract(first_chip, wide, 1, 1))
    drop = contract(second_coeff, wide, 1, 0)
    drop_low, drop_high = drop[:own], drop[own:]
    mine = jnp.where(core == 0, drop_low, drop_high)
    theirs = jnp.where(core == 0, drop_high, drop_low)
    first_own = jnp.where(core == 0, first_chip[:own], first_chip[own:])
    second = first_own - (mine + shift(theirs, "core", 1))
    second_parts = transposed(second)

    coeff_slots = (first_coeff + second_coeff).reshape(2 * own, nx, brows)
    coeff_slots = jnp.roll(coeff_slots.transpose(1, 0, 2), xi, axis=0)
    packed = jnp.concatenate(
        [
            jnp.broadcast_to(second[None], (nx, own, nodes)),
            coeff_slots.reshape(nx, -1, nodes),
        ],
        axis=1,
    )
    landed = lax.all_to_all(packed, "x", 0, 0, tiled=True)
    coeffs = landed[:, own:].reshape(nx * 2 * own, brows).T
    same = landed[:, :own]
    across = shift(same, "core", 1)
    both = jnp.where(
        core == 0,
        jnp.stack([same, across], axis=1),
        jnp.stack([across, same], axis=1),
    )
    second_all = both.reshape(nx * 2 * own, nodes)
    second_g, second_c = [finish(p) for p in second_parts]

    rows = jnp.concatenate([basis_g, basis_c, second, second_g, second_c], axis=0)
    piece = sum_rows_to_piece(contract(second_all, rows, 1, 1))
    ports_piece = piece.shape[0]
    narrow = spread(piece[:, 2 * brows :], ("x", "core"))
    narrow = narrow.reshape(2 * nx, ports_piece, 3, own).transpose(1, 2, 0, 3)
    full = piece_to_rows(
        jnp.concatenate(
            [piece[:, : 2 * brows], narrow.reshape(ports_piece, -1)], axis=1
        )
    )
    ports = 2 * nx * own
    g_rows = full[:, :brows]
    c_rows = full[:, brows : 2 * brows]
    gram, g_core, c_core = [
        full[:, 2 * brows + i * ports : 2 * brows + (i + 1) * ports] for i in range(3)
    ]
    factor = jnp.linalg.cholesky(gram)
    identity = jnp.eye(ports, dtype=factor.dtype)
    inverse = jax.scipy.linalg.solve_triangular(factor, identity, lower=True)
    inverse_own = lax.dynamic_slice_in_dim(inverse, col * own, own, 0)
    chol_rows = lax.dynamic_slice_in_dim(factor, col * own, own, 0)
    new_block = contract(inverse_own, second_all, 1, 0)
    g_proj = contract(g_rows, inverse, 0, 1)
    c_proj = contract(c_rows, inverse, 0, 1)
    g_new = contract(contract(inverse_own, g_core, 1, 1), inverse, 1, 1)
    c_new = contract(contract(inverse_own, c_core, 1, 1), inverse, 1, 1)
    return (new_block, coeffs, chol_rows, port_proj, g_proj, c_proj, g_new, c_new)


def solution(mesh):
    sizes = (8, 8, 4, 2) if mesh.devices.size == 512 else (2, 2, 4, 2)
    fine = Mesh(mesh.devices.reshape(sizes), ("z", "y", "x", "core"))
    dom, col = ("z", "y"), ("x", "core")
    placed = (
        P(col, dom),
        P(col, dom),
        P(dom, None, None, None),
        P(dom, None, None, None),
        P(dom, None),
        P(dom),
        P(dom),
        P(),
    )
    return jax.shard_map(
        on_device,
        mesh=fine,
        in_specs=placed,
        out_specs=(P(col, dom),) + (P(col, None),) * 7,
        check_vma=False,
    )
```

```python
import functools

import jax
import jax.numpy as jnp
from jax import lax
from jax.experimental import pallas as pl
from jax.experimental.pallas import tpu as pltpu
from jax.sharding import Mesh
from jax.sharding import PartitionSpec as P

EXACT = lax.Precision.HIGHEST
HIGH = lax.Precision.HIGH
DOM = ("z", "y")


def contract(left, right, left_dim, right_dim, precision=HIGH):
    return lax.dot_general(
        left, right, (((left_dim,), (right_dim,)), ((), ())), precision=precision
    )


def exact(left, right, left_dim, right_dim):
    return contract(left, right, left_dim, right_dim, EXACT)


def shift(value, axis, step):
    size = lax.axis_size(axis)
    return lax.ppermute(value, axis, [(i, (i + step) % size) for i in range(size)])


def shift_open(value, axis, step):
    size = lax.axis_size(axis)
    pairs = [(i, i + step) for i in range(size) if 0 <= i + step < size]
    return lax.ppermute(value, axis, pairs)


def scatter_sum(pieces, axis):
    return jnp.sum(lax.all_to_all(pieces, axis, 0, 0, tiled=True), axis=0)


def spread(piece, axis):
    size = lax.axis_size(axis)
    copies = jnp.broadcast_to(piece[None], (size,) + piece.shape)
    return lax.all_to_all(copies, axis, 0, 0, tiled=True)


def sum_rows_to_piece(value):
    parts = lax.axis_size(DOM)
    rows, lanes = value.shape
    return scatter_sum(value.reshape(parts, rows // parts, lanes), DOM)


def piece_to_rows(piece):
    return spread(piece, DOM).reshape(-1, piece.shape[1])


def sum_dom(value):
    parts = lax.axis_size(DOM)
    rows, lanes = value.shape
    tiles = value.reshape(rows // 8, 8, lanes // 128, 128).transpose(0, 2, 1, 3)
    piece = scatter_sum(tiles.reshape(parts, -1, 128), DOM)
    full = spread(piece, DOM).reshape(rows // 8, lanes // 128, 8, 128)
    return full.transpose(0, 2, 1, 3).reshape(rows, lanes)


def dense_tiles(tiles, tile_cols, width):
    count, nbrs, rows, cols = tiles.shape
    hit = tile_cols[:, :, None] == jnp.arange(width, dtype=jnp.int32)
    total = 0.0
    for k in range(nbrs):
        total = total + jnp.where(
            hit[:, k, None, :, None], tiles[:, k, :, None, :], 0.0
        )
    return total.reshape(count * rows, width * cols)

EDGE = 64


def finish_kernel(own, brows, col_ref, full_ref, second_ref, *refs):
    outs, (work, factor, inverse) = refs[:6], refs[6:]
    new_ref, chol_ref, g_proj_ref, c_proj_ref, g_new_ref, c_new_ref = outs
    ports = full_ref.shape[0]
    at = 2 * brows
    gram = full_ref[:, at : at + ports]
    work[...] = 0.5 * (gram + gram.T)
    factor[...] = jnp.zeros_like(factor)
    inverse[...] = jnp.zeros_like(inverse)
    row_ids = lax.broadcasted_iota(jnp.int32, (EDGE, 2 * EDGE), 0)
    lane_ids = lax.broadcasted_iota(jnp.int32, (EDGE, 2 * EDGE), 1)
    eye = (lane_ids - EDGE == row_ids).astype(jnp.float32)
    for k in range(ports // EDGE):
        lo, hi = k * EDGE, (k + 1) * EDGE
        pair = jnp.concatenate([work[lo:hi, lo:hi], eye[:, EDGE:]], axis=1)
        for j in range(EDGE - 1):
            top = (j + 1) // 8 * 8
            pivot = pair[j : j + 1, :]
            scale = pair[top:, j : j + 1] / pair[j : j + 1, j : j + 1]
            scale = jnp.where(row_ids[top:, :1] > j, scale, 0.0)
            rest = pair[top:] - scale * pivot
            pair = rest if top == 0 else jnp.concatenate([pair[:top], rest], axis=0)
        diag = jnp.sum(
            jnp.where(lane_ids == row_ids, pair, 0.0), axis=1, keepdims=True
        )
        pair = pair * lax.rsqrt(diag)
        upper = jnp.where(
            lane_ids[:, :EDGE] >= row_ids[:, :EDGE], pair[:, :EDGE], 0.0
        )
        small = pair[:, EDGE:]
        factor[lo:hi, lo:hi] = upper.T
        if hi < ports:
            panel = exact(work[hi:, lo:hi], small, 1, 1)
            factor[hi:, lo:hi] = panel
            work[hi:, hi:] = work[hi:, hi:] - exact(panel, panel, 1, 1)
        start = (
            lax.broadcasted_iota(jnp.int32, (EDGE, ports), 1)
            == lax.broadcasted_iota(jnp.int32, (EDGE, ports), 0) + lo
        ).astype(jnp.float32)
        if k > 0:
            start = start - exact(factor[lo:hi, :lo], inverse[:lo, :], 1, 0)
        inverse[lo:hi, :] = exact(small, start, 1, 0)
    rows = pl.ds(pl.multiple_of(col_ref[0] * own, own), own)
    full_inverse = inverse[...]
    inverse_own = inverse[rows, :]
    chol_ref[...] = factor[rows, :]
    new_ref[...] = exact(inverse_own, second_ref[...], 1, 0)
    g_proj_ref[...] = exact(full_ref[:, :brows].T, full_inverse, 1, 1)
    c_proj_ref[...] = exact(full_ref[:, brows:at].T, full_inverse, 1, 1)
    for i, out_ref in ((1, g_new_ref), (2, c_new_ref)):
        core = full_ref[:, at + i * ports : at + (i + 1) * ports]
        out_ref[...] = exact(
            exact(inverse_own, core, 1, 1), full_inverse, 1, 1
        )


def finish_block(col, full, second_all, own, brows):
    ports, nodes = second_all.shape
    f32 = jnp.float32
    vmem = pl.BlockSpec(memory_space=pltpu.VMEM)
    return pl.pallas_call(
        functools.partial(finish_kernel, own, brows),
        out_shape=(
            jax.ShapeDtypeStruct((own, nodes), f32),
            jax.ShapeDtypeStruct((own, ports), f32),
            jax.ShapeDtypeStruct((brows, ports), f32),
            jax.ShapeDtypeStruct((brows, ports), f32),
            jax.ShapeDtypeStruct((own, ports), f32),
            jax.ShapeDtypeStruct((own, ports), f32),
        ),
        in_specs=[pl.BlockSpec(memory_space=pltpu.SMEM), vmem, vmem],
        out_specs=(vmem,) * 6,
        scratch_shapes=[pltpu.VMEM((ports, ports), f32)] * 3,
        name="finish_block",
    )(col[None].astype(jnp.int32), full, second_all)


def on_device(block, basis, g_tiles, c_tiles, tile_cols, bnd_rows, dinv, port_nodes):
    tile = g_tiles.shape[-1]
    nodes = block.shape[1]
    own = block.shape[0]
    brows = basis.shape[0]
    width = nodes // tile + 2
    nx = lax.axis_size("x")
    xi = lax.axis_index("x")
    core = lax.axis_index("core")
    dom = lax.axis_index(DOM)
    col = xi * 2 + core
    half = brows // 2

    right = shift(basis, "x", -1)
    left = shift(basis, "x", 1)
    far_low = shift(left[:half], "x", 1)
    far_high = shift(right[half:], "x", -1)
    wide = jnp.concatenate([basis, right, far_low, far_high, left], axis=0)

    node_ids = jnp.arange(nodes, dtype=jnp.int32)
    edge_hot = (bnd_rows[:, None] == node_ids[None, :]).astype(jnp.float32)
    port_hot = ((port_nodes - dom * nodes)[:, None] == node_ids[None, :]).astype(
        jnp.float32
    )

    rim = contract(block, edge_hot, 1, 1)
    before = shift_open(rim, DOM, 1)
    after = shift_open(rim, DOM, -1)
    g_dense = dense_tiles(g_tiles, tile_cols, width)
    c_dense = dense_tiles(c_tiles, tile_cols, width)
    extended = jnp.concatenate([block, before, after], axis=1)
    work = dinv[None, :] * contract(extended, c_dense, 1, 1)
    other = shift(work, "core", 1)
    low = jnp.where(core == 0, work, other)
    high = jnp.where(core == 0, other, work)
    work_chip = jnp.concatenate([low, high], axis=0)

    def transposed(rows):
        fulls = [contract(rows, dense, 1, 0) for dense in (g_dense, c_dense)]
        both = jnp.concatenate([f[:, nodes:] for f in fulls], axis=0)
        back = shift_open(both[:, :tile], DOM, -1)
        ahead = shift_open(both[:, tile:], DOM, 1)
        return fulls, back, ahead

    def finish(parts):
        fulls, back, ahead = parts
        count = fulls[0].shape[0]
        rim_sum = contract(back + ahead, edge_hot, 1, 0)
        return [f[:, :nodes] + rim_sum[i * count : (i + 1) * count] for i, f in enumerate(fulls)]

    basis_parts = transposed(basis)
    port_piece = sum_rows_to_piece(exact(port_hot, basis, 1, 1))
    port_proj = piece_to_rows(port_piece).T
    basis_g, basis_c = finish(basis_parts)

    work_chip, port_proj = lax.optimization_barrier((work_chip, port_proj))

    first_coeff = sum_dom(contract(work_chip, wide, 1, 1))
    drop = contract(first_coeff, wide, 1, 0)
    first_chip = work_chip - (drop + shift(drop, "core", 1))
    second_coeff = sum_dom(contract(first_chip, wide, 1, 1))
    drop = contract(second_coeff, wide, 1, 0)
    drop_low, drop_high = drop[:own], drop[own:]
    mine = jnp.where(core == 0, drop_low, drop_high)
    theirs = jnp.where(core == 0, drop_high, drop_low)
    first_own = jnp.where(core == 0, first_chip[:own], first_chip[own:])
    second = first_own - (mine + shift(theirs, "core", 1))
    second_parts = transposed(second)

    coeff_slots = (first_coeff + second_coeff).reshape(2 * own, nx, brows)
    coeff_slots = jnp.roll(coeff_slots.transpose(1, 0, 2), xi, axis=0)
    packed = jnp.concatenate(
        [
            jnp.broadcast_to(second[None], (nx, own, nodes)),
            coeff_slots.reshape(nx, -1, nodes),
        ],
        axis=1,
    )
    landed = lax.all_to_all(packed, "x", 0, 0, tiled=True)
    coeffs = landed[:, own:].reshape(nx * 2 * own, brows).T
    same = landed[:, :own]
    across = shift(same, "core", 1)
    both = jnp.where(
        core == 0,
        jnp.stack([same, across], axis=1),
        jnp.stack([across, same], axis=1),
    )
    second_all = both.reshape(nx * 2 * own, nodes)
    second_g, second_c = finish(second_parts)

    rows = jnp.concatenate([basis_g, basis_c, second, second_g, second_c], axis=0)
    piece = sum_rows_to_piece(contract(second_all, rows, 1, 1))
    ports_piece = piece.shape[0]
    narrow = spread(piece[:, 2 * brows :], ("x", "core"))
    narrow = narrow.reshape(2 * nx, ports_piece, 3, own).transpose(1, 2, 0, 3)
    full = piece_to_rows(
        jnp.concatenate(
            [piece[:, : 2 * brows], narrow.reshape(ports_piece, -1)], axis=1
        )
    )
    ports = 2 * nx * own
    new_block, chol_rows, g_proj, c_proj, g_new, c_new = finish_block(
        col, full, second_all, own, brows
    )
    return (new_block, coeffs, chol_rows, port_proj, g_proj, c_proj, g_new, c_new)


def solution(mesh):
    sizes = (8, 8, 4, 2) if mesh.devices.size == 512 else (2, 2, 4, 2)
    fine = Mesh(mesh.devices.reshape(sizes), ("z", "y", "x", "core"))
    dom, col = ("z", "y"), ("x", "core")
    placed = (
        P(col, dom),
        P(col, dom),
        P(dom, None, None, None),
        P(dom, None, None, None),
        P(dom, None),
        P(dom),
        P(dom),
        P(),
    )
    return jax.shard_map(
        on_device,
        mesh=fine,
        in_specs=placed,
        out_specs=(P(col, dom),) + (P(col, None),) * 7,
        check_vma=False,
    )
```

```python
import functools

import jax
import jax.numpy as jnp
from jax import lax
from jax.experimental import pallas as pl
from jax.experimental.pallas import tpu as pltpu
from jax.sharding import Mesh
from jax.sharding import PartitionSpec as P

EXACT = lax.Precision.HIGHEST
HIGH = lax.Precision.HIGH
DOM = ("z", "y")


def contract(left, right, left_dim, right_dim, precision=HIGH):
    return lax.dot_general(
        left, right, (((left_dim,), (right_dim,)), ((), ())), precision=precision
    )


def exact(left, right, left_dim, right_dim):
    return contract(left, right, left_dim, right_dim, EXACT)


def shift(value, axis, step):
    size = lax.axis_size(axis)
    return lax.ppermute(value, axis, [(i, (i + step) % size) for i in range(size)])


def shift_open(value, axis, step):
    size = lax.axis_size(axis)
    pairs = [(i, i + step) for i in range(size) if 0 <= i + step < size]
    return lax.ppermute(value, axis, pairs)


def scatter_sum(pieces, axis):
    return jnp.sum(lax.all_to_all(pieces, axis, 0, 0, tiled=True), axis=0)


def spread(piece, axis):
    size = lax.axis_size(axis)
    copies = jnp.broadcast_to(piece[None], (size,) + piece.shape)
    return lax.all_to_all(copies, axis, 0, 0, tiled=True)


def sum_rows_to_piece(value):
    parts = lax.axis_size(DOM)
    rows, lanes = value.shape
    return scatter_sum(value.reshape(parts, rows // parts, lanes), DOM)


def piece_to_rows(piece):
    return spread(piece, DOM).reshape(-1, piece.shape[1])


def sum_dom(value):
    parts = lax.axis_size(DOM)
    rows, lanes = value.shape
    tiles = value.reshape(rows // 8, 8, lanes // 128, 128).transpose(0, 2, 1, 3)
    piece = scatter_sum(tiles.reshape(parts, -1, 128), DOM)
    full = spread(piece, DOM).reshape(rows // 8, lanes // 128, 8, 128)
    return full.transpose(0, 2, 1, 3).reshape(rows, lanes)


def split(value):
    high = value.astype(jnp.bfloat16)
    low = (value - high.astype(jnp.float32)).astype(jnp.bfloat16)
    return high, low


def three_pass(left, right, left_dim, right_dim):
    dims = (((left_dim,), (right_dim,)), ((), ()))
    f32 = jnp.float32
    rows = left[0].shape[0]
    stacked = jnp.concatenate(left, axis=0)
    main = lax.dot_general(stacked, right[0], dims, preferred_element_type=f32)
    side = lax.dot_general(left[0], right[1], dims, preferred_element_type=f32)
    return main[:rows] + (main[rows:] + side)


def act_kernel(cols_ref, rows_ref, g_ref, c_ref, local_ref, back_ref, ahead_ref, acc):
    count, nbrs, tile, _ = g_ref.shape
    rows = rows_ref.shape[0]
    acc[...] = jnp.zeros_like(acc)

    def step(t, carry):
        left = split(rows_ref[:, pl.ds(pl.multiple_of(t * tile, tile), tile)])
        for i, ref in enumerate((g_ref, c_ref)):
            for k in range(nbrs):
                part = three_pass(left, split(ref[t, k]), 1, 0)
                at = cols_ref[t, k]
                acc[at, i * rows : (i + 1) * rows, :] += part
        return carry

    lax.fori_loop(0, count, step, 0)
    for t in range(count):
        local_ref[:, t * tile : (t + 1) * tile] = acc[t]
    back_ref[...] = acc[count]
    ahead_ref[...] = acc[count + 1]


def transposed_action(tile_cols, rows, g_tiles, c_tiles):
    count, nbrs, tile, _ = g_tiles.shape
    num, nodes = rows.shape
    vmem = pl.BlockSpec(memory_space=pltpu.VMEM)
    f32 = jnp.float32
    return pl.pallas_call(
        act_kernel,
        out_shape=(
            jax.ShapeDtypeStruct((2 * num, nodes), f32),
            jax.ShapeDtypeStruct((2 * num, tile), f32),
            jax.ShapeDtypeStruct((2 * num, tile), f32),
        ),
        in_specs=[pl.BlockSpec(memory_space=pltpu.SMEM), vmem, vmem, vmem],
        out_specs=(vmem,) * 3,
        scratch_shapes=[pltpu.VMEM((count + 2, 2 * num, tile), f32)],
        name="transposed_action",
    )(tile_cols, rows, g_tiles, c_tiles)


def work_kernel(cols_ref, block_ref, before_ref, after_ref, c_ref, dinv_ref, out_ref, ext):
    count, nbrs, tile, _ = c_ref.shape
    for t in range(count):
        ext[t] = block_ref[:, t * tile : (t + 1) * tile]
    ext[count] = before_ref[...]
    ext[count + 1] = after_ref[...]
    for t in range(count):
        total = 0.0
        for k in range(nbrs):
            left = split(ext[cols_ref[t, k]])
            total = total + three_pass(left, split(c_ref[t, k]), 1, 1)
        lanes = slice(t * tile, (t + 1) * tile)
        out_ref[:, lanes] = dinv_ref[:, lanes] * total


def scaled_action(tile_cols, block, before, after, c_tiles, dinv):
    count, nbrs, tile, _ = c_tiles.shape
    vmem = pl.BlockSpec(memory_space=pltpu.VMEM)
    return pl.pallas_call(
        work_kernel,
        out_shape=jax.ShapeDtypeStruct(block.shape, jnp.float32),
        in_specs=[pl.BlockSpec(memory_space=pltpu.SMEM)] + [vmem] * 5,
        out_specs=vmem,
        scratch_shapes=[pltpu.VMEM((count + 2, block.shape[0], tile), jnp.float32)],
        name="scaled_action",
    )(tile_cols, block, before, after, c_tiles, dinv[None, :])


def first_kernel(work_ref, *refs):
    pieces, (coeff_ref, high_ref, low_ref) = refs[:-3], refs[-3:]
    left = split(work_ref[...])
    at = 0
    for ref in pieces:
        rows = ref.shape[0]
        right = split(ref[...])
        high_ref[at : at + rows, :] = right[0]
        low_ref[at : at + rows, :] = right[1]
        coeff_ref[:, at : at + rows] = three_pass(left, right, 1, 1)
        at += rows


def first_coefficients(work, pieces):
    rows = sum(p.shape[0] for p in pieces)
    vmem = pl.BlockSpec(memory_space=pltpu.VMEM)
    bf16 = jnp.bfloat16
    return pl.pallas_call(
        first_kernel,
        out_shape=(
            jax.ShapeDtypeStruct((work.shape[0], rows), jnp.float32),
            jax.ShapeDtypeStruct((rows, work.shape[1]), bf16),
            jax.ShapeDtypeStruct((rows, work.shape[1]), bf16),
        ),
        in_specs=[vmem] * (1 + len(pieces)),
        out_specs=(vmem,) * 3,
        name="first_coefficients",
    )(work, *pieces)


def product_kernel(right_dim, left_ref, high_ref, low_ref, out_ref):
    right = (high_ref[...], low_ref[...])
    out_ref[...] = three_pass(split(left_ref[...]), right, 1, right_dim)


def wide_product(left, high, low, right_dim):
    vmem = pl.BlockSpec(memory_space=pltpu.VMEM)
    cols = high.shape[1 - right_dim]
    return pl.pallas_call(
        functools.partial(product_kernel, right_dim),
        out_shape=jax.ShapeDtypeStruct((left.shape[0], cols), jnp.float32),
        in_specs=[vmem] * 3,
        out_specs=vmem,
        name="wide_product",
    )(left, high, low)


def pair_kernel(
    core_ref, same_ref, across_ref, basis_ref, second_ref, local_ref, back_ref,
    ahead_ref, edge_ref, out_ref, all_ref
):
    core = core_ref[0]
    nx, own, nodes = same_ref.shape
    for i in range(nx):
        all_ref[2 * i + core] = same_ref[i]
        all_ref[2 * i + 1 - core] = across_ref[i]
    ports = 2 * nx * own
    left = split(all_ref[...].reshape(ports, nodes))
    rim = split(back_ref[...] + ahead_ref[...])
    hot = edge_ref[...].astype(jnp.bfloat16)
    dims = (((1,), (0,)), ((), ()))
    f32 = jnp.float32
    image = local_ref[...] + (
        lax.dot_general(rim[0], hot, dims, preferred_element_type=f32)
        + lax.dot_general(rim[1], hot, dims, preferred_element_type=f32)
    )
    wide = basis_ref.shape[0]
    out_ref[:, :wide] = three_pass(left, split(basis_ref[...]), 1, 1)
    tail = jnp.concatenate([second_ref[...], image], axis=0)
    out_ref[:, wide:] = three_pass(left, split(tail), 1, 1)


def pair_products(core, same, across, basis_images, second, local, back, ahead, edge_hot):
    nx, own, nodes = same.shape
    ports = 2 * nx * own
    vmem = pl.BlockSpec(memory_space=pltpu.VMEM)
    f32 = jnp.float32
    lanes = basis_images.shape[0] + 3 * own
    out, all_rows = pl.pallas_call(
        pair_kernel,
        out_shape=(
            jax.ShapeDtypeStruct((ports, lanes), f32),
            jax.ShapeDtypeStruct((2 * nx, own, nodes), f32),
        ),
        in_specs=[pl.BlockSpec(memory_space=pltpu.SMEM)] + [vmem] * 8,
        out_specs=(vmem,) * 2,
        name="pair_products",
    )(core[None].astype(jnp.int32), same, across, basis_images, second, local, back, ahead, edge_hot)
    return out, all_rows.reshape(ports, nodes)


EDGE = 64


def factor_kernel(own, col_ref, gram_ref, second_ref, new_ref, chol_ref, inverse, work, factor):
    ports = gram_ref.shape[0]
    gram = gram_ref[...]
    work[...] = 0.5 * (gram + gram.T)
    factor[...] = jnp.zeros_like(factor)
    inverse[...] = jnp.zeros_like(inverse)
    row_ids = lax.broadcasted_iota(jnp.int32, (EDGE, 2 * EDGE), 0)
    lane_ids = lax.broadcasted_iota(jnp.int32, (EDGE, 2 * EDGE), 1)
    eye = (lane_ids - EDGE == row_ids).astype(jnp.float32)
    for k in range(ports // EDGE):
        lo, hi = k * EDGE, (k + 1) * EDGE
        pair = jnp.concatenate([work[lo:hi, lo:hi], eye[:, EDGE:]], axis=1)
        for j in range(EDGE - 1):
            top = (j + 1) // 8 * 8
            pivot = pair[j : j + 1, :]
            scale = pair[top:, j : j + 1] / pair[j : j + 1, j : j + 1]
            scale = jnp.where(row_ids[top:, :1] > j, scale, 0.0)
            rest = pair[top:] - scale * pivot
            pair = rest if top == 0 else jnp.concatenate([pair[:top], rest], axis=0)
        diag = jnp.sum(
            jnp.where(lane_ids == row_ids, pair, 0.0), axis=1, keepdims=True
        )
        pair = pair * lax.rsqrt(diag)
        upper = jnp.where(
            lane_ids[:, :EDGE] >= row_ids[:, :EDGE], pair[:, :EDGE], 0.0
        )
        small = pair[:, EDGE:]
        factor[lo:hi, lo:hi] = upper.T
        if hi < ports:
            panel = exact(work[hi:, lo:hi], small, 1, 1)
            factor[hi:, lo:hi] = panel
            work[hi:, hi:] = work[hi:, hi:] - exact(panel, panel, 1, 1)
        start = (
            lax.broadcasted_iota(jnp.int32, (EDGE, ports), 1)
            == lax.broadcasted_iota(jnp.int32, (EDGE, ports), 0) + lo
        ).astype(jnp.float32)
        if k > 0:
            start = start - exact(factor[lo:hi, :lo], inverse[:lo, :], 1, 0)
        inverse[lo:hi, :] = exact(small, start, 1, 0)
    rows = pl.ds(pl.multiple_of(col_ref[0] * own, own), own)
    chol_ref[...] = factor[rows, :]
    new_ref[...] = exact(inverse[rows, :], second_ref[...], 1, 0)


def factor_block(col, gram, second_all, own):
    ports, nodes = second_all.shape
    f32 = jnp.float32
    vmem = pl.BlockSpec(memory_space=pltpu.VMEM)
    return pl.pallas_call(
        functools.partial(factor_kernel, own),
        out_shape=(
            jax.ShapeDtypeStruct((own, nodes), f32),
            jax.ShapeDtypeStruct((own, ports), f32),
            jax.ShapeDtypeStruct((ports, ports), f32),
        ),
        in_specs=[pl.BlockSpec(memory_space=pltpu.SMEM), vmem, vmem],
        out_specs=(vmem,) * 3,
        scratch_shapes=[pltpu.VMEM((ports, ports), f32)] * 2,
        cost_estimate=pl.CostEstimate(
            flops=20_000_000_000, transcendentals=0, bytes_accessed=2_000_000
        ),
        name="factor_block",
    )(col, gram, second_all)


def finish_kernel(own, brows, col_ref, full_ref, inverse_ref, *outs):
    g_proj_ref, c_proj_ref, g_new_ref, c_new_ref = outs
    ports = full_ref.shape[0]
    rows = pl.ds(pl.multiple_of(col_ref[0] * own, own), own)
    inverse = inverse_ref[...]
    inverse_own = inverse_ref[rows, :]
    g_proj_ref[...] = exact(full_ref[:, :brows].T, inverse, 1, 1)
    c_proj_ref[...] = exact(full_ref[:, brows : 2 * brows].T, inverse, 1, 1)
    for i, out_ref in enumerate((g_new_ref, c_new_ref)):
        at = 2 * brows + i * ports
        core = full_ref[:, at : at + ports]
        out_ref[...] = exact(exact(inverse_own, core, 1, 1), inverse, 1, 1)


def finish_block(col, full, inverse, own, brows):
    ports = inverse.shape[0]
    f32 = jnp.float32
    vmem = pl.BlockSpec(memory_space=pltpu.VMEM)
    return pl.pallas_call(
        functools.partial(finish_kernel, own, brows),
        out_shape=(
            jax.ShapeDtypeStruct((brows, ports), f32),
            jax.ShapeDtypeStruct((brows, ports), f32),
            jax.ShapeDtypeStruct((own, ports), f32),
            jax.ShapeDtypeStruct((own, ports), f32),
        ),
        in_specs=[pl.BlockSpec(memory_space=pltpu.SMEM), vmem, vmem],
        out_specs=(vmem,) * 4,
        name="finish_block",
    )(col, full, inverse)


def on_device(block, basis, g_tiles, c_tiles, tile_cols, bnd_rows, dinv, port_nodes):
    tile = g_tiles.shape[-1]
    nodes = block.shape[1]
    own = block.shape[0]
    brows = basis.shape[0]
    width = nodes // tile + 2
    nx = lax.axis_size("x")
    xi = lax.axis_index("x")
    core = lax.axis_index("core")
    dom = lax.axis_index(DOM)
    col = xi * 2 + core
    half = brows // 2

    right = shift(basis, "x", -1)
    left = shift(basis, "x", 1)
    far_low = shift(left[:half], "x", 1)
    far_high = shift(right[half:], "x", -1)

    node_ids = jnp.arange(nodes, dtype=jnp.int32)
    edge_hot = (bnd_rows[:, None] == node_ids[None, :]).astype(jnp.float32)
    port_hot = ((port_nodes - dom * nodes)[:, None] == node_ids[None, :]).astype(
        jnp.float32
    )

    rim = contract(block, edge_hot, 1, 1)
    before = shift_open(rim, DOM, 1)
    after = shift_open(rim, DOM, -1)
    work = scaled_action(tile_cols, block, before, after, c_tiles, dinv)
    other = shift(work, "core", 1)
    low = jnp.where(core == 0, work, other)
    high = jnp.where(core == 0, other, work)
    work_chip = jnp.concatenate([low, high], axis=0)

    def exchange(back, ahead):
        return shift_open(back, DOM, -1), shift_open(ahead, DOM, 1)

    port_proj = piece_to_rows(sum_rows_to_piece(exact(port_hot, basis, 1, 1))).T
    work_chip, port_proj = lax.optimization_barrier((work_chip, port_proj))

    partial, high_rows, low_rows = first_coefficients(
        work_chip, (basis, right, far_low, far_high, left)
    )
    partial, basis_rows = lax.optimization_barrier((partial, basis))
    basis_local, basis_back, basis_ahead = transposed_action(
        tile_cols, basis_rows, g_tiles, c_tiles
    )
    basis_back, basis_ahead = exchange(basis_back, basis_ahead)
    basis_images = basis_local + contract(basis_back + basis_ahead, edge_hot, 1, 0)
    first_coeff = sum_dom(partial)
    drop = wide_product(first_coeff, high_rows, low_rows, 0)
    first_chip = work_chip - (drop + shift(drop, "core", 1))
    first_chip, basis_images = lax.optimization_barrier((first_chip, basis_images))
    second_coeff = sum_dom(wide_product(first_chip, high_rows, low_rows, 1))
    drop = wide_product(second_coeff, high_rows, low_rows, 0)
    drop_low, drop_high = drop[:own], drop[own:]
    mine = jnp.where(core == 0, drop_low, drop_high)
    theirs = jnp.where(core == 0, drop_high, drop_low)
    first_own = jnp.where(core == 0, first_chip[:own], first_chip[own:])
    second = first_own - (mine + shift(theirs, "core", 1))

    local, back, ahead = transposed_action(tile_cols, second, g_tiles, c_tiles)
    back, ahead = exchange(back, ahead)

    same = spread(second, "x")
    same, local = lax.optimization_barrier((same, local))
    across = shift(same, "core", 1)
    products, second_all = pair_products(
        core, same, across, basis_images, second, local, back, ahead, edge_hot
    )
    products, coeff_sum = lax.optimization_barrier(
        (products, first_coeff + second_coeff)
    )
    piece = sum_rows_to_piece(products)

    slots = coeff_sum.reshape(2 * own, nx, brows)
    landed = [slots[:, 0]] + [shift(slots[:, k], "x", k) for k in range(1, nx)]
    landed = jnp.roll(jnp.stack(landed[::-1]), xi + 1, axis=0)
    coeffs = landed.reshape(nx * 2 * own, brows).T

    ports_piece = piece.shape[0]
    ports = 2 * nx * own
    narrow = spread(piece[:, 2 * brows :], ("x", "core"))
    narrow = narrow.reshape(2 * nx, ports_piece, 3, own).transpose(1, 2, 0, 3)
    narrow = narrow.reshape(ports_piece, 3 * ports)
    gram = piece_to_rows(narrow[:, :ports])
    rest = jnp.concatenate([piece[:, : 2 * brows], narrow[:, ports:]], axis=1)
    gram, rest = lax.optimization_barrier((gram, rest))
    full = piece_to_rows(rest)
    where = col[None].astype(jnp.int32)
    new_block, chol_rows, inverse = factor_block(where, gram, second_all, own)
    g_proj, c_proj, g_new, c_new = finish_block(where, full, inverse, own, brows)
    return (new_block, coeffs, chol_rows, port_proj, g_proj, c_proj, g_new, c_new)


def solution(mesh):
    sizes = (8, 8, 4, 2) if mesh.devices.size == 512 else (2, 2, 4, 2)
    fine = Mesh(mesh.devices.reshape(sizes), ("z", "y", "x", "core"))
    dom, col = ("z", "y"), ("x", "core")
    placed = (
        P(col, dom),
        P(col, dom),
        P(dom, None, None, None),
        P(dom, None, None, None),
        P(dom, None),
        P(dom),
        P(dom),
        P(),
    )
    return jax.shard_map(
        on_device,
        mesh=fine,
        in_specs=placed,
        out_specs=(P(col, dom),) + (P(col, None),) * 7,
        check_vma=False,
    )
```

```python
import functools

import jax
import jax.numpy as jnp
from jax import lax
from jax.experimental import pallas as pl
from jax.experimental.pallas import tpu as pltpu
from jax.sharding import Mesh
from jax.sharding import PartitionSpec as P

EXACT = lax.Precision.HIGHEST
HIGH = lax.Precision.HIGH
DOM = ("z", "y")


def contract(left, right, left_dim, right_dim, precision=HIGH):
    return lax.dot_general(
        left, right, (((left_dim,), (right_dim,)), ((), ())), precision=precision
    )


def exact(left, right, left_dim, right_dim):
    return contract(left, right, left_dim, right_dim, EXACT)


def shift(value, axis, step):
    size = lax.axis_size(axis)
    return lax.ppermute(value, axis, [(i, (i + step) % size) for i in range(size)])


def shift_open(value, axis, step):
    size = lax.axis_size(axis)
    pairs = [(i, i + step) for i in range(size) if 0 <= i + step < size]
    return lax.ppermute(value, axis, pairs)


def scatter_sum(pieces, axis):
    return jnp.sum(lax.all_to_all(pieces, axis, 0, 0, tiled=True), axis=0)


def spread(piece, axis):
    size = lax.axis_size(axis)
    copies = jnp.broadcast_to(piece[None], (size,) + piece.shape)
    return lax.all_to_all(copies, axis, 0, 0, tiled=True)


def sum_rows_to_piece(value):
    parts = lax.axis_size(DOM)
    rows, lanes = value.shape
    return scatter_sum(value.reshape(parts, rows // parts, lanes), DOM)


def piece_to_rows(piece):
    return spread(piece, DOM).reshape(-1, piece.shape[1])


def sum_dom(*values):
    parts = lax.axis_size(DOM)
    tiles = []
    for value in values:
        rows, lanes = value.shape
        split_up = value.reshape(rows // 8, 8, lanes // 128, 128).transpose(0, 2, 1, 3)
        tiles.append(split_up.reshape(parts, -1, 128))
    full = spread(scatter_sum(jnp.concatenate(tiles, axis=1), DOM), DOM)
    sums, at = [], 0
    for value, tile in zip(values, tiles):
        rows, lanes = value.shape
        own = full[:, at : at + tile.shape[1]]
        at += tile.shape[1]
        own = own.reshape(rows // 8, lanes // 128, 8, 128).transpose(0, 2, 1, 3)
        sums.append(own.reshape(rows, lanes))
    return sums[0] if len(sums) == 1 else sums


def split(value):
    high = value.astype(jnp.bfloat16)
    low = (value - high.astype(jnp.float32)).astype(jnp.bfloat16)
    return high, low


def three_pass(left, right, left_dim, right_dim):
    dims = (((left_dim,), (right_dim,)), ((), ()))
    f32 = jnp.float32
    rows = left[0].shape[0]
    stacked = jnp.concatenate(left, axis=0)
    main = lax.dot_general(stacked, right[0], dims, preferred_element_type=f32)
    side = lax.dot_general(left[0], right[1], dims, preferred_element_type=f32)
    return main[:rows] + (main[rows:] + side)


def act_kernel(cols_ref, rows_ref, g_ref, c_ref, local_ref, back_ref, ahead_ref, acc):
    count, nbrs, tile, _ = g_ref.shape
    rows = rows_ref.shape[0]
    acc[...] = jnp.zeros_like(acc)

    def step(t, carry):
        left = split(rows_ref[:, pl.ds(pl.multiple_of(t * tile, tile), tile)])
        for i, ref in enumerate((g_ref, c_ref)):
            for k in range(nbrs):
                part = three_pass(left, split(ref[t, k]), 1, 0)
                at = cols_ref[t, k]
                acc[at, i * rows : (i + 1) * rows, :] += part
        return carry

    lax.fori_loop(0, count, step, 0)
    for t in range(count):
        local_ref[:, t * tile : (t + 1) * tile] = acc[t]
    back_ref[...] = acc[count]
    ahead_ref[...] = acc[count + 1]


def transposed_action(tile_cols, rows, g_tiles, c_tiles):
    count, nbrs, tile, _ = g_tiles.shape
    num, nodes = rows.shape
    vmem = pl.BlockSpec(memory_space=pltpu.VMEM)
    f32 = jnp.float32
    return pl.pallas_call(
        act_kernel,
        out_shape=(
            jax.ShapeDtypeStruct((2 * num, nodes), f32),
            jax.ShapeDtypeStruct((2 * num, tile), f32),
            jax.ShapeDtypeStruct((2 * num, tile), f32),
        ),
        in_specs=[pl.BlockSpec(memory_space=pltpu.SMEM), vmem, vmem, vmem],
        out_specs=(vmem,) * 3,
        scratch_shapes=[pltpu.VMEM((count + 2, 2 * num, tile), f32)],
        name="transposed_action",
    )(tile_cols, rows, g_tiles, c_tiles)


def work_kernel(cols_ref, block_ref, before_ref, after_ref, c_ref, dinv_ref, out_ref, ext):
    count, nbrs, tile, _ = c_ref.shape
    for t in range(count):
        ext[t] = block_ref[:, t * tile : (t + 1) * tile]
    ext[count] = before_ref[...]
    ext[count + 1] = after_ref[...]
    for t in range(count):
        total = 0.0
        for k in range(nbrs):
            left = split(ext[cols_ref[t, k]])
            total = total + three_pass(left, split(c_ref[t, k]), 1, 1)
        lanes = slice(t * tile, (t + 1) * tile)
        out_ref[:, lanes] = dinv_ref[:, lanes] * total


def scaled_action(tile_cols, block, before, after, c_tiles, dinv):
    count, nbrs, tile, _ = c_tiles.shape
    vmem = pl.BlockSpec(memory_space=pltpu.VMEM)
    return pl.pallas_call(
        work_kernel,
        out_shape=jax.ShapeDtypeStruct(block.shape, jnp.float32),
        in_specs=[pl.BlockSpec(memory_space=pltpu.SMEM)] + [vmem] * 5,
        out_specs=vmem,
        scratch_shapes=[pltpu.VMEM((count + 2, block.shape[0], tile), jnp.float32)],
        name="scaled_action",
    )(tile_cols, block, before, after, c_tiles, dinv[None, :])


def first_kernel(work_ref, *refs):
    pieces, (coeff_ref, high_ref, low_ref) = refs[:-3], refs[-3:]
    left = split(work_ref[...])
    at = 0
    for ref in pieces:
        rows = ref.shape[0]
        right = split(ref[...])
        high_ref[at : at + rows, :] = right[0]
        low_ref[at : at + rows, :] = right[1]
        coeff_ref[:, at : at + rows] = three_pass(left, right, 1, 1)
        at += rows


def first_coefficients(work, pieces):
    rows = sum(p.shape[0] for p in pieces)
    vmem = pl.BlockSpec(memory_space=pltpu.VMEM)
    bf16 = jnp.bfloat16
    return pl.pallas_call(
        first_kernel,
        out_shape=(
            jax.ShapeDtypeStruct((work.shape[0], rows), jnp.float32),
            jax.ShapeDtypeStruct((rows, work.shape[1]), bf16),
            jax.ShapeDtypeStruct((rows, work.shape[1]), bf16),
        ),
        in_specs=[vmem] * (1 + len(pieces)),
        out_specs=(vmem,) * 3,
        name="first_coefficients",
    )(work, *pieces)


def product_kernel(right_dim, left_ref, high_ref, low_ref, out_ref):
    right = (high_ref[...], low_ref[...])
    out_ref[...] = three_pass(split(left_ref[...]), right, 1, right_dim)


def wide_product(left, high, low, right_dim):
    vmem = pl.BlockSpec(memory_space=pltpu.VMEM)
    cols = high.shape[1 - right_dim]
    return pl.pallas_call(
        functools.partial(product_kernel, right_dim),
        out_shape=jax.ShapeDtypeStruct((left.shape[0], cols), jnp.float32),
        in_specs=[vmem] * 3,
        out_specs=vmem,
        name="wide_product",
    )(left, high, low)


def pair_kernel(
    core_ref, same_ref, across_ref, basis_ref, second_ref, local_ref, back_ref,
    ahead_ref, edge_ref, out_ref, all_ref
):
    core = core_ref[0]
    nx, own, nodes = same_ref.shape
    for i in range(nx):
        all_ref[2 * i + core] = same_ref[i]
        all_ref[2 * i + 1 - core] = across_ref[i]
    ports = 2 * nx * own
    left = split(all_ref[...].reshape(ports, nodes))
    rim = split(back_ref[...] + ahead_ref[...])
    hot = edge_ref[...].astype(jnp.bfloat16)
    dims = (((1,), (0,)), ((), ()))
    f32 = jnp.float32
    image = local_ref[...] + (
        lax.dot_general(rim[0], hot, dims, preferred_element_type=f32)
        + lax.dot_general(rim[1], hot, dims, preferred_element_type=f32)
    )
    wide = basis_ref.shape[0]
    out_ref[:, :wide] = three_pass(left, split(basis_ref[...]), 1, 1)
    tail = jnp.concatenate([second_ref[...], image], axis=0)
    out_ref[:, wide:] = three_pass(left, split(tail), 1, 1)


def pair_products(core, same, across, basis_images, second, local, back, ahead, edge_hot):
    nx, own, nodes = same.shape
    ports = 2 * nx * own
    vmem = pl.BlockSpec(memory_space=pltpu.VMEM)
    f32 = jnp.float32
    lanes = basis_images.shape[0] + 3 * own
    out, all_rows = pl.pallas_call(
        pair_kernel,
        out_shape=(
            jax.ShapeDtypeStruct((ports, lanes), f32),
            jax.ShapeDtypeStruct((2 * nx, own, nodes), f32),
        ),
        in_specs=[pl.BlockSpec(memory_space=pltpu.SMEM)] + [vmem] * 8,
        out_specs=(vmem,) * 2,
        name="pair_products",
    )(core[None].astype(jnp.int32), same, across, basis_images, second, local, back, ahead, edge_hot)
    return out, all_rows.reshape(ports, nodes)


EDGE = 64


def factor_kernel(own, col_ref, gram_ref, second_ref, new_ref, chol_ref, inverse, work, factor):
    ports = gram_ref.shape[0]
    gram = gram_ref[...]
    work[...] = 0.5 * (gram + gram.T)
    factor[...] = jnp.zeros_like(factor)
    inverse[...] = jnp.zeros_like(inverse)
    row_ids = lax.broadcasted_iota(jnp.int32, (EDGE, 2 * EDGE), 0)
    lane_ids = lax.broadcasted_iota(jnp.int32, (EDGE, 2 * EDGE), 1)
    eye = (lane_ids - EDGE == row_ids).astype(jnp.float32)
    for k in range(ports // EDGE):
        lo, hi = k * EDGE, (k + 1) * EDGE
        pair = jnp.concatenate([work[lo:hi, lo:hi], eye[:, EDGE:]], axis=1)
        for j in range(EDGE - 1):
            group = j // 8 * 8
            pivot = pair[j : j + 1, :]
            pivot = pivot * (1.0 / pivot[:, j : j + 1])
            column = pair[group : group + 8, j : j + 1]
            column = jnp.where(row_ids[group : group + 8, :1] > j, column, 0.0)
            parts = [pair[group : group + 8] - column * pivot]
            if group > 0:
                parts.insert(0, pair[:group])
            if group + 8 < EDGE:
                rest = pair[group + 8 :]
                parts.append(rest - rest[:, j : j + 1] * pivot)
            pair = jnp.concatenate(parts, axis=0)
        diag = jnp.sum(
            jnp.where(lane_ids == row_ids, pair, 0.0), axis=1, keepdims=True
        )
        pair = pair * lax.rsqrt(diag)
        upper = jnp.where(
            lane_ids[:, :EDGE] >= row_ids[:, :EDGE], pair[:, :EDGE], 0.0
        )
        small = pair[:, EDGE:]
        factor[lo:hi, lo:hi] = upper.T
        if hi < ports:
            panel = exact(work[hi:, lo:hi], small, 1, 1)
            factor[hi:, lo:hi] = panel
            work[hi:, hi:] = work[hi:, hi:] - exact(panel, panel, 1, 1)
        start = (
            lax.broadcasted_iota(jnp.int32, (EDGE, ports), 1)
            == lax.broadcasted_iota(jnp.int32, (EDGE, ports), 0) + lo
        ).astype(jnp.float32)
        if k > 0:
            start = start - exact(factor[lo:hi, :lo], inverse[:lo, :], 1, 0)
        inverse[lo:hi, :] = exact(small, start, 1, 0)
    rows = pl.ds(pl.multiple_of(col_ref[0] * own, own), own)
    chol_ref[...] = factor[rows, :]
    new_ref[...] = exact(inverse[rows, :], second_ref[...], 1, 0)


def factor_block(col, gram, second_all, own):
    ports, nodes = second_all.shape
    f32 = jnp.float32
    vmem = pl.BlockSpec(memory_space=pltpu.VMEM)
    return pl.pallas_call(
        functools.partial(factor_kernel, own),
        out_shape=(
            jax.ShapeDtypeStruct((own, nodes), f32),
            jax.ShapeDtypeStruct((own, ports), f32),
            jax.ShapeDtypeStruct((ports, ports), f32),
        ),
        in_specs=[pl.BlockSpec(memory_space=pltpu.SMEM), vmem, vmem],
        out_specs=(vmem,) * 3,
        scratch_shapes=[pltpu.VMEM((ports, ports), f32)] * 2,
        cost_estimate=pl.CostEstimate(
            flops=20_000_000_000, transcendentals=0, bytes_accessed=2_000_000
        ),
        name="factor_block",
    )(col, gram, second_all)


def finish_kernel(own, brows, col_ref, full_ref, inverse_ref, *outs):
    g_proj_ref, c_proj_ref, g_new_ref, c_new_ref = outs
    ports = full_ref.shape[0]
    rows = pl.ds(pl.multiple_of(col_ref[0] * own, own), own)
    inverse = inverse_ref[...]
    inverse_own = inverse_ref[rows, :]
    g_proj_ref[...] = exact(full_ref[:, :brows].T, inverse, 1, 1)
    c_proj_ref[...] = exact(full_ref[:, brows : 2 * brows].T, inverse, 1, 1)
    for i, out_ref in enumerate((g_new_ref, c_new_ref)):
        at = 2 * brows + i * ports
        core = full_ref[:, at : at + ports]
        out_ref[...] = exact(exact(inverse_own, core, 1, 1), inverse, 1, 1)


def finish_block(col, full, inverse, own, brows):
    ports = inverse.shape[0]
    f32 = jnp.float32
    vmem = pl.BlockSpec(memory_space=pltpu.VMEM)
    return pl.pallas_call(
        functools.partial(finish_kernel, own, brows),
        out_shape=(
            jax.ShapeDtypeStruct((brows, ports), f32),
            jax.ShapeDtypeStruct((brows, ports), f32),
            jax.ShapeDtypeStruct((own, ports), f32),
            jax.ShapeDtypeStruct((own, ports), f32),
        ),
        in_specs=[pl.BlockSpec(memory_space=pltpu.SMEM), vmem, vmem],
        out_specs=(vmem,) * 4,
        name="finish_block",
    )(col, full, inverse)


def on_device(block, basis, g_tiles, c_tiles, tile_cols, bnd_rows, dinv, port_nodes):
    tile = g_tiles.shape[-1]
    nodes = block.shape[1]
    own = block.shape[0]
    brows = basis.shape[0]
    width = nodes // tile + 2
    nx = lax.axis_size("x")
    xi = lax.axis_index("x")
    core = lax.axis_index("core")
    dom = lax.axis_index(DOM)
    col = xi * 2 + core
    half = brows // 2

    right = shift(basis, "x", -1)
    left = shift(basis, "x", 1)
    far_low = shift(left[:half], "x", 1)
    far_high = shift(right[half:], "x", -1)

    node_ids = jnp.arange(nodes, dtype=jnp.int32)
    edge_hot = (bnd_rows[:, None] == node_ids[None, :]).astype(jnp.float32)
    port_hot = ((port_nodes - dom * nodes)[:, None] == node_ids[None, :]).astype(
        jnp.float32
    )

    rim = contract(block, edge_hot, 1, 1)
    before = shift_open(rim, DOM, 1)
    after = shift_open(rim, DOM, -1)
    work = scaled_action(tile_cols, block, before, after, c_tiles, dinv)
    other = shift(work, "core", 1)
    low = jnp.where(core == 0, work, other)
    high = jnp.where(core == 0, other, work)
    work_chip = jnp.concatenate([low, high], axis=0)

    def exchange(back, ahead):
        return shift_open(back, DOM, -1), shift_open(ahead, DOM, 1)

    port_part = exact(port_hot, basis, 1, 1)
    work_chip, port_part = lax.optimization_barrier((work_chip, port_part))

    partial, high_rows, low_rows = first_coefficients(
        work_chip, (basis, right, far_low, far_high, left)
    )
    partial, basis_rows = lax.optimization_barrier((partial, basis))
    basis_local, basis_back, basis_ahead = transposed_action(
        tile_cols, basis_rows, g_tiles, c_tiles
    )
    basis_back, basis_ahead = exchange(basis_back, basis_ahead)
    basis_images = basis_local + contract(basis_back + basis_ahead, edge_hot, 1, 0)
    first_coeff, port_sum = sum_dom(partial, port_part)
    port_proj = port_sum.T
    drop = wide_product(first_coeff, high_rows, low_rows, 0)
    first_chip = work_chip - (drop + shift(drop, "core", 1))
    second_coeff = sum_dom(wide_product(first_chip, high_rows, low_rows, 1))
    drop = wide_product(second_coeff, high_rows, low_rows, 0)
    drop_low, drop_high = drop[:own], drop[own:]
    mine = jnp.where(core == 0, drop_low, drop_high)
    theirs = jnp.where(core == 0, drop_high, drop_low)
    first_own = jnp.where(core == 0, first_chip[:own], first_chip[own:])
    second = first_own - (mine + shift(theirs, "core", 1))
    second, basis_images = lax.optimization_barrier((second, basis_images))

    local, back, ahead = transposed_action(tile_cols, second, g_tiles, c_tiles)
    back, ahead = exchange(back, ahead)

    same = spread(second, "x")
    same, back, ahead = lax.optimization_barrier((same, back, ahead))
    across = shift(same, "core", 1)
    products, second_all = pair_products(
        core, same, across, basis_images, second, local, back, ahead, edge_hot
    )
    products, coeff_sum = lax.optimization_barrier(
        (products, first_coeff + second_coeff)
    )
    piece = sum_rows_to_piece(products)

    slots = coeff_sum.reshape(2 * own, nx, brows)
    landed = [slots[:, 0]] + [shift(slots[:, k], "x", k) for k in range(1, nx)]
    landed = jnp.roll(jnp.stack(landed[::-1]), xi + 1, axis=0)
    coeffs = landed.reshape(nx * 2 * own, brows).T

    ports_piece = piece.shape[0]
    ports = 2 * nx * own
    narrow = spread(piece[:, 2 * brows :], ("x", "core"))
    narrow = narrow.reshape(2 * nx, ports_piece, 3, own).transpose(1, 2, 0, 3)
    narrow = narrow.reshape(ports_piece, 3 * ports)
    gram = piece_to_rows(narrow[:, :ports])
    rest = jnp.concatenate([piece[:, : 2 * brows], narrow[:, ports:]], axis=1)
    gram, rest = lax.optimization_barrier((gram, rest))
    full = piece_to_rows(rest)
    where = col[None].astype(jnp.int32)
    new_block, chol_rows, inverse = factor_block(where, gram, second_all, own)
    g_proj, c_proj, g_new, c_new = finish_block(where, full, inverse, own, brows)
    return (new_block, coeffs, chol_rows, port_proj, g_proj, c_proj, g_new, c_new)


def solution(mesh):
    sizes = (8, 8, 4, 2) if mesh.devices.size == 512 else (2, 2, 4, 2)
    fine = Mesh(mesh.devices.reshape(sizes), ("z", "y", "x", "core"))
    dom, col = ("z", "y"), ("x", "core")
    placed = (
        P(col, dom),
        P(col, dom),
        P(dom, None, None, None),
        P(dom, None, None, None),
        P(dom, None),
        P(dom),
        P(dom),
        P(),
    )
    return jax.shard_map(
        on_device,
        mesh=fine,
        in_specs=placed,
        out_specs=(P(col, dom),) + (P(col, None),) * 7,
        check_vma=False,
    )
```

```python
import functools

import jax
import jax.numpy as jnp
from jax import lax
from jax.experimental import pallas as pl
from jax.experimental.pallas import tpu as pltpu
from jax.sharding import Mesh
from jax.sharding import PartitionSpec as P

EXACT = lax.Precision.HIGHEST
HIGH = lax.Precision.HIGH
DOM = ("z", "y")


def contract(left, right, left_dim, right_dim, precision=HIGH):
    return lax.dot_general(
        left, right, (((left_dim,), (right_dim,)), ((), ())), precision=precision
    )


def exact(left, right, left_dim, right_dim):
    return contract(left, right, left_dim, right_dim, EXACT)


def shift(value, axis, step):
    size = lax.axis_size(axis)
    return lax.ppermute(value, axis, [(i, (i + step) % size) for i in range(size)])


def shift_open(value, axis, step):
    size = lax.axis_size(axis)
    pairs = [(i, i + step) for i in range(size) if 0 <= i + step < size]
    return lax.ppermute(value, axis, pairs)


def scatter_sum(pieces, axis):
    return jnp.sum(lax.all_to_all(pieces, axis, 0, 0, tiled=True), axis=0)


def spread(piece, axis):
    size = lax.axis_size(axis)
    copies = jnp.broadcast_to(piece[None], (size,) + piece.shape)
    return lax.all_to_all(copies, axis, 0, 0, tiled=True)


def sum_rows_to_piece(value):
    parts = lax.axis_size(DOM)
    rows, lanes = value.shape
    return scatter_sum(value.reshape(parts, rows // parts, lanes), DOM)


def piece_to_rows(piece):
    return spread(piece, DOM).reshape(-1, piece.shape[1])


def sum_dom(*values, beside=None):
    parts = lax.axis_size(DOM)
    tiles = []
    for value in values:
        rows, lanes = value.shape
        split_up = value.reshape(rows // 8, 8, lanes // 128, 128).transpose(0, 2, 1, 3)
        tiles.append(split_up.reshape(parts, -1, 128))
    piece = scatter_sum(jnp.concatenate(tiles, axis=1), DOM)
    if beside is not None:
        piece, beside = lax.optimization_barrier((piece, beside))
    full = spread(piece, DOM)
    sums, at = [], 0
    for value, tile in zip(values, tiles):
        rows, lanes = value.shape
        own = full[:, at : at + tile.shape[1]]
        at += tile.shape[1]
        own = own.reshape(rows // 8, lanes // 128, 8, 128).transpose(0, 2, 1, 3)
        sums.append(own.reshape(rows, lanes))
    return sums if beside is None else (sums, beside)


def split(value):
    high = value.astype(jnp.bfloat16)
    low = (value - high.astype(jnp.float32)).astype(jnp.bfloat16)
    return high, low


def three_pass(left, right, left_dim, right_dim):
    dims = (((left_dim,), (right_dim,)), ((), ()))
    f32 = jnp.float32
    rows = left[0].shape[0]
    stacked = jnp.concatenate(left, axis=0)
    main = lax.dot_general(stacked, right[0], dims, preferred_element_type=f32)
    side = lax.dot_general(left[0], right[1], dims, preferred_element_type=f32)
    return main[:rows] + (main[rows:] + side)


def act_kernel(cols_ref, rows_ref, g_ref, c_ref, local_ref, back_ref, ahead_ref, acc):
    count, nbrs, tile, _ = g_ref.shape
    rows = rows_ref.shape[0]
    acc[...] = jnp.zeros_like(acc)

    def step(t, carry):
        left = split(rows_ref[:, pl.ds(pl.multiple_of(t * tile, tile), tile)])
        for i, ref in enumerate((g_ref, c_ref)):
            for k in range(nbrs):
                part = three_pass(left, split(ref[t, k]), 1, 0)
                at = cols_ref[t, k]
                acc[at, i * rows : (i + 1) * rows, :] += part
        return carry

    lax.fori_loop(0, count, step, 0)
    for t in range(count):
        local_ref[:, t * tile : (t + 1) * tile] = acc[t]
    back_ref[...] = acc[count]
    ahead_ref[...] = acc[count + 1]


def transposed_action(tile_cols, rows, g_tiles, c_tiles):
    count, nbrs, tile, _ = g_tiles.shape
    num, nodes = rows.shape
    vmem = pl.BlockSpec(memory_space=pltpu.VMEM)
    f32 = jnp.float32
    return pl.pallas_call(
        act_kernel,
        out_shape=(
            jax.ShapeDtypeStruct((2 * num, nodes), f32),
            jax.ShapeDtypeStruct((2 * num, tile), f32),
            jax.ShapeDtypeStruct((2 * num, tile), f32),
        ),
        in_specs=[pl.BlockSpec(memory_space=pltpu.SMEM), vmem, vmem, vmem],
        out_specs=(vmem,) * 3,
        scratch_shapes=[pltpu.VMEM((count + 2, 2 * num, tile), f32)],
        name="transposed_action",
    )(tile_cols, rows, g_tiles, c_tiles)


def work_kernel(cols_ref, block_ref, before_ref, after_ref, c_ref, dinv_ref, out_ref, ext):
    count, nbrs, tile, _ = c_ref.shape
    for t in range(count):
        ext[t] = block_ref[:, t * tile : (t + 1) * tile]
    ext[count] = before_ref[...]
    ext[count + 1] = after_ref[...]
    for t in range(count):
        total = 0.0
        for k in range(nbrs):
            left = split(ext[cols_ref[t, k]])
            total = total + three_pass(left, split(c_ref[t, k]), 1, 1)
        lanes = slice(t * tile, (t + 1) * tile)
        out_ref[:, lanes] = dinv_ref[:, lanes] * total


def scaled_action(tile_cols, block, before, after, c_tiles, dinv):
    count, nbrs, tile, _ = c_tiles.shape
    vmem = pl.BlockSpec(memory_space=pltpu.VMEM)
    return pl.pallas_call(
        work_kernel,
        out_shape=jax.ShapeDtypeStruct(block.shape, jnp.float32),
        in_specs=[pl.BlockSpec(memory_space=pltpu.SMEM)] + [vmem] * 5,
        out_specs=vmem,
        scratch_shapes=[pltpu.VMEM((count + 2, block.shape[0], tile), jnp.float32)],
        name="scaled_action",
    )(tile_cols, block, before, after, c_tiles, dinv[None, :])


def first_kernel(work_ref, *refs):
    pieces, (coeff_ref, high_ref, low_ref) = refs[:-3], refs[-3:]
    left = split(work_ref[...])
    at = 0
    for ref in pieces:
        rows = ref.shape[0]
        right = split(ref[...])
        high_ref[at : at + rows, :] = right[0]
        low_ref[at : at + rows, :] = right[1]
        coeff_ref[:, at : at + rows] = three_pass(left, right, 1, 1)
        at += rows


def first_coefficients(work, pieces):
    rows = sum(p.shape[0] for p in pieces)
    vmem = pl.BlockSpec(memory_space=pltpu.VMEM)
    bf16 = jnp.bfloat16
    return pl.pallas_call(
        first_kernel,
        out_shape=(
            jax.ShapeDtypeStruct((work.shape[0], rows), jnp.float32),
            jax.ShapeDtypeStruct((rows, work.shape[1]), bf16),
            jax.ShapeDtypeStruct((rows, work.shape[1]), bf16),
        ),
        in_specs=[vmem] * (1 + len(pieces)),
        out_specs=(vmem,) * 3,
        name="first_coefficients",
    )(work, *pieces)


def product_kernel(right_dim, left_ref, high_ref, low_ref, out_ref):
    right = (high_ref[...], low_ref[...])
    out_ref[...] = three_pass(split(left_ref[...]), right, 1, right_dim)


def wide_product(left, high, low, right_dim):
    vmem = pl.BlockSpec(memory_space=pltpu.VMEM)
    cols = high.shape[1 - right_dim]
    return pl.pallas_call(
        functools.partial(product_kernel, right_dim),
        out_shape=jax.ShapeDtypeStruct((left.shape[0], cols), jnp.float32),
        in_specs=[vmem] * 3,
        out_specs=vmem,
        name="wide_product",
    )(left, high, low)


def pair_kernel(
    core_ref, same_ref, across_ref, basis_ref, second_ref, local_ref, back_ref,
    ahead_ref, edge_ref, out_ref, all_ref
):
    core = core_ref[0]
    nx, own, nodes = same_ref.shape
    for i in range(nx):
        all_ref[2 * i + core] = same_ref[i]
        all_ref[2 * i + 1 - core] = across_ref[i]
    ports = 2 * nx * own
    left = split(all_ref[...].reshape(ports, nodes))
    rim = split(back_ref[...] + ahead_ref[...])
    hot = edge_ref[...].astype(jnp.bfloat16)
    dims = (((1,), (0,)), ((), ()))
    f32 = jnp.float32
    image = local_ref[...] + (
        lax.dot_general(rim[0], hot, dims, preferred_element_type=f32)
        + lax.dot_general(rim[1], hot, dims, preferred_element_type=f32)
    )
    wide = basis_ref.shape[0]
    out_ref[:, :wide] = three_pass(left, split(basis_ref[...]), 1, 1)
    tail = jnp.concatenate([second_ref[...], image], axis=0)
    out_ref[:, wide:] = three_pass(left, split(tail), 1, 1)


def pair_products(core, same, across, basis_images, second, local, back, ahead, edge_hot):
    nx, own, nodes = same.shape
    ports = 2 * nx * own
    vmem = pl.BlockSpec(memory_space=pltpu.VMEM)
    f32 = jnp.float32
    lanes = basis_images.shape[0] + 3 * own
    out, all_rows = pl.pallas_call(
        pair_kernel,
        out_shape=(
            jax.ShapeDtypeStruct((ports, lanes), f32),
            jax.ShapeDtypeStruct((2 * nx, own, nodes), f32),
        ),
        in_specs=[pl.BlockSpec(memory_space=pltpu.SMEM)] + [vmem] * 8,
        out_specs=(vmem,) * 2,
        name="pair_products",
    )(core[None].astype(jnp.int32), same, across, basis_images, second, local, back, ahead, edge_hot)
    return out, all_rows.reshape(ports, nodes)


EDGE = 64


def factor_kernel(own, col_ref, gram_ref, second_ref, new_ref, chol_ref, inverse, work, factor):
    ports = gram_ref.shape[0]
    gram = gram_ref[...]
    work[...] = 0.5 * (gram + gram.T)
    factor[...] = jnp.zeros_like(factor)
    inverse[...] = jnp.zeros_like(inverse)
    row_ids = lax.broadcasted_iota(jnp.int32, (EDGE, 2 * EDGE), 0)
    lane_ids = lax.broadcasted_iota(jnp.int32, (EDGE, 2 * EDGE), 1)
    eye = (lane_ids - EDGE == row_ids).astype(jnp.float32)
    for k in range(ports // EDGE):
        lo, hi = k * EDGE, (k + 1) * EDGE
        pair = jnp.concatenate([work[lo:hi, lo:hi], eye[:, EDGE:]], axis=1)
        for j in range(EDGE - 1):
            group = j // 8 * 8
            pivot = pair[j : j + 1, :]
            pivot = pivot * (1.0 / pivot[:, j : j + 1])
            column = pair[group : group + 8, j : j + 1]
            column = jnp.where(row_ids[group : group + 8, :1] > j, column, 0.0)
            parts = [pair[group : group + 8] - column * pivot]
            if group > 0:
                parts.insert(0, pair[:group])
            if group + 8 < EDGE:
                rest = pair[group + 8 :]
                parts.append(rest - rest[:, j : j + 1] * pivot)
            pair = jnp.concatenate(parts, axis=0)
        diag = jnp.sum(
            jnp.where(lane_ids == row_ids, pair, 0.0), axis=1, keepdims=True
        )
        pair = pair * lax.rsqrt(diag)
        upper = jnp.where(
            lane_ids[:, :EDGE] >= row_ids[:, :EDGE], pair[:, :EDGE], 0.0
        )
        small = pair[:, EDGE:]
        factor[lo:hi, lo:hi] = upper.T
        if hi < ports:
            panel = exact(work[hi:, lo:hi], small, 1, 1)
            factor[hi:, lo:hi] = panel
            work[hi:, hi:] = work[hi:, hi:] - exact(panel, panel, 1, 1)
        start = (
            lax.broadcasted_iota(jnp.int32, (EDGE, ports), 1)
            == lax.broadcasted_iota(jnp.int32, (EDGE, ports), 0) + lo
        ).astype(jnp.float32)
        if k > 0:
            start = start - exact(factor[lo:hi, :lo], inverse[:lo, :], 1, 0)
        inverse[lo:hi, :] = exact(small, start, 1, 0)
    rows = pl.ds(pl.multiple_of(col_ref[0] * own, own), own)
    chol_ref[...] = factor[rows, :]
    new_ref[...] = exact(inverse[rows, :], second_ref[...], 1, 0)


def factor_block(col, gram, second_all, own):
    ports, nodes = second_all.shape
    f32 = jnp.float32
    vmem = pl.BlockSpec(memory_space=pltpu.VMEM)
    return pl.pallas_call(
        functools.partial(factor_kernel, own),
        out_shape=(
            jax.ShapeDtypeStruct((own, nodes), f32),
            jax.ShapeDtypeStruct((own, ports), f32),
            jax.ShapeDtypeStruct((ports, ports), f32),
        ),
        in_specs=[pl.BlockSpec(memory_space=pltpu.SMEM), vmem, vmem],
        out_specs=(vmem,) * 3,
        scratch_shapes=[pltpu.VMEM((ports, ports), f32)] * 2,
        cost_estimate=pl.CostEstimate(
            flops=20_000_000_000, transcendentals=0, bytes_accessed=2_000_000
        ),
        name="factor_block",
    )(col, gram, second_all)


def finish_kernel(own, brows, col_ref, full_ref, inverse_ref, *outs):
    g_proj_ref, c_proj_ref, g_new_ref, c_new_ref = outs
    ports = full_ref.shape[0]
    rows = pl.ds(pl.multiple_of(col_ref[0] * own, own), own)
    inverse = inverse_ref[...]
    inverse_own = inverse_ref[rows, :]
    g_proj_ref[...] = exact(full_ref[:, :brows].T, inverse, 1, 1)
    c_proj_ref[...] = exact(full_ref[:, brows : 2 * brows].T, inverse, 1, 1)
    for i, out_ref in enumerate((g_new_ref, c_new_ref)):
        at = 2 * brows + i * ports
        core = full_ref[:, at : at + ports]
        out_ref[...] = exact(exact(inverse_own, core, 1, 1), inverse, 1, 1)


def finish_block(col, full, inverse, own, brows):
    ports = inverse.shape[0]
    f32 = jnp.float32
    vmem = pl.BlockSpec(memory_space=pltpu.VMEM)
    return pl.pallas_call(
        functools.partial(finish_kernel, own, brows),
        out_shape=(
            jax.ShapeDtypeStruct((brows, ports), f32),
            jax.ShapeDtypeStruct((brows, ports), f32),
            jax.ShapeDtypeStruct((own, ports), f32),
            jax.ShapeDtypeStruct((own, ports), f32),
        ),
        in_specs=[pl.BlockSpec(memory_space=pltpu.SMEM), vmem, vmem],
        out_specs=(vmem,) * 4,
        name="finish_block",
    )(col, full, inverse)


def on_device(block, basis, g_tiles, c_tiles, tile_cols, bnd_rows, dinv, port_nodes):
    tile = g_tiles.shape[-1]
    nodes = block.shape[1]
    own = block.shape[0]
    brows = basis.shape[0]
    width = nodes // tile + 2
    nx = lax.axis_size("x")
    xi = lax.axis_index("x")
    core = lax.axis_index("core")
    dom = lax.axis_index(DOM)
    col = xi * 2 + core
    half = brows // 2

    right = shift(basis, "x", -1)
    left = shift(basis, "x", 1)
    far_low = shift(left[:half], "x", 1)
    far_high = shift(right[half:], "x", -1)

    node_ids = jnp.arange(nodes, dtype=jnp.int32)
    edge_hot = (bnd_rows[:, None] == node_ids[None, :]).astype(jnp.float32)
    port_hot = ((port_nodes - dom * nodes)[:, None] == node_ids[None, :]).astype(
        jnp.float32
    )

    rim = contract(block, edge_hot, 1, 1)
    before = shift_open(rim, DOM, 1)
    after = shift_open(rim, DOM, -1)
    work = scaled_action(tile_cols, block, before, after, c_tiles, dinv)
    other = shift(work, "core", 1)
    low = jnp.where(core == 0, work, other)
    high = jnp.where(core == 0, other, work)
    work_chip = jnp.concatenate([low, high], axis=0)

    def exchange(back, ahead):
        return shift_open(back, DOM, -1), shift_open(ahead, DOM, 1)

    port_part = exact(port_hot, basis, 1, 1)
    work_chip, port_part = lax.optimization_barrier((work_chip, port_part))

    partial, high_rows, low_rows = first_coefficients(
        work_chip, (basis, right, far_low, far_high, left)
    )
    partial, basis_rows = lax.optimization_barrier((partial, basis))
    basis_local, basis_back, basis_ahead = transposed_action(
        tile_cols, basis_rows, g_tiles, c_tiles
    )
    first_coeff, port_sum = sum_dom(partial, port_part)
    first_coeff, basis_local, basis_back, basis_ahead = lax.optimization_barrier(
        (first_coeff, basis_local, basis_back, basis_ahead)
    )
    basis_rims = exchange(basis_back, basis_ahead)
    port_proj = port_sum.T
    drop = wide_product(first_coeff, high_rows, low_rows, 0)
    first_chip = work_chip - (drop + shift(drop, "core", 1))
    (second_coeff,), basis_rims = sum_dom(
        wide_product(first_chip, high_rows, low_rows, 1), beside=basis_rims
    )
    basis_images = basis_local + contract(sum(basis_rims), edge_hot, 1, 0)
    drop = wide_product(second_coeff, high_rows, low_rows, 0)
    drop_low, drop_high = drop[:own], drop[own:]
    mine = jnp.where(core == 0, drop_low, drop_high)
    theirs = jnp.where(core == 0, drop_high, drop_low)
    first_own = jnp.where(core == 0, first_chip[:own], first_chip[own:])
    second = first_own - (mine + shift(theirs, "core", 1))
    second, basis_images = lax.optimization_barrier((second, basis_images))

    local, back, ahead = transposed_action(tile_cols, second, g_tiles, c_tiles)
    back, ahead = exchange(back, ahead)

    same = spread(second, "x")
    same, back, ahead = lax.optimization_barrier((same, back, ahead))
    across = shift(same, "core", 1)
    products, second_all = pair_products(
        core, same, across, basis_images, second, local, back, ahead, edge_hot
    )
    products, coeff_sum = lax.optimization_barrier(
        (products, first_coeff + second_coeff)
    )
    piece = sum_rows_to_piece(products)

    slots = coeff_sum.reshape(2 * own, nx, brows)
    landed = [slots[:, 0]] + [shift(slots[:, k], "x", k) for k in range(1, nx)]
    landed = jnp.roll(jnp.stack(landed[::-1]), xi + 1, axis=0)
    coeffs = landed.reshape(nx * 2 * own, brows).T

    ports_piece = piece.shape[0]
    ports = 2 * nx * own
    narrow = spread(piece[:, 2 * brows :], ("x", "core"))
    narrow = narrow.reshape(2 * nx, ports_piece, 3, own).transpose(1, 2, 0, 3)
    narrow = narrow.reshape(ports_piece, 3 * ports)
    gram = piece_to_rows(narrow[:, :ports])
    rest = jnp.concatenate([piece[:, : 2 * brows], narrow[:, ports:]], axis=1)
    gram, rest = lax.optimization_barrier((gram, rest))
    full = piece_to_rows(rest)
    where = col[None].astype(jnp.int32)
    new_block, chol_rows, inverse = factor_block(where, gram, second_all, own)
    g_proj, c_proj, g_new, c_new = finish_block(where, full, inverse, own, brows)
    return (new_block, coeffs, chol_rows, port_proj, g_proj, c_proj, g_new, c_new)


def solution(mesh):
    sizes = (8, 8, 4, 2) if mesh.devices.size == 512 else (2, 2, 4, 2)
    fine = Mesh(mesh.devices.reshape(sizes), ("z", "y", "x", "core"))
    dom, col = ("z", "y"), ("x", "core")
    placed = (
        P(col, dom),
        P(col, dom),
        P(dom, None, None, None),
        P(dom, None, None, None),
        P(dom, None),
        P(dom),
        P(dom),
        P(),
    )
    return jax.shard_map(
        on_device,
        mesh=fine,
        in_specs=placed,
        out_specs=(P(col, dom),) + (P(col, None),) * 7,
        check_vma=False,
    )
```

```python
import functools

import jax
import jax.numpy as jnp
from jax import lax
from jax.experimental import pallas as pl
from jax.experimental.pallas import tpu as pltpu
from jax.sharding import Mesh
from jax.sharding import PartitionSpec as P

EXACT = lax.Precision.HIGHEST
HIGH = lax.Precision.HIGH
DOM = ("z", "y")


def contract(left, right, left_dim, right_dim, precision=HIGH):
    return lax.dot_general(
        left, right, (((left_dim,), (right_dim,)), ((), ())), precision=precision
    )


def exact(left, right, left_dim, right_dim):
    return contract(left, right, left_dim, right_dim, EXACT)


def shift(value, axis, step):
    size = lax.axis_size(axis)
    return lax.ppermute(value, axis, [(i, (i + step) % size) for i in range(size)])


def shift_open(value, axis, step):
    size = lax.axis_size(axis)
    pairs = [(i, i + step) for i in range(size) if 0 <= i + step < size]
    return lax.ppermute(value, axis, pairs)


def scatter_sum(pieces, axis):
    return jnp.sum(lax.all_to_all(pieces, axis, 0, 0, tiled=True), axis=0)


def spread(piece, axis):
    size = lax.axis_size(axis)
    copies = jnp.broadcast_to(piece[None], (size,) + piece.shape)
    return lax.all_to_all(copies, axis, 0, 0, tiled=True)


def sum_rows_to_piece(value):
    parts = lax.axis_size(DOM)
    rows, lanes = value.shape
    return scatter_sum(value.reshape(parts, rows // parts, lanes), DOM)


def piece_to_rows(piece):
    return spread(piece, DOM).reshape(-1, piece.shape[1])


def sum_dom(*values, beside=None):
    parts = lax.axis_size(DOM)
    tiles = []
    for value in values:
        rows, lanes = value.shape
        split_up = value.reshape(rows // 8, 8, lanes // 128, 128).transpose(0, 2, 1, 3)
        tiles.append(split_up.reshape(parts, -1, 128))
    piece = scatter_sum(jnp.concatenate(tiles, axis=1), DOM)
    if beside is not None:
        piece, beside = lax.optimization_barrier((piece, beside))
    full = spread(piece, DOM)
    sums, at = [], 0
    for value, tile in zip(values, tiles):
        rows, lanes = value.shape
        own = full[:, at : at + tile.shape[1]]
        at += tile.shape[1]
        own = own.reshape(rows // 8, lanes // 128, 8, 128).transpose(0, 2, 1, 3)
        sums.append(own.reshape(rows, lanes))
    return sums if beside is None else (sums, beside)


def split(value):
    high = value.astype(jnp.bfloat16)
    low = (value - high.astype(jnp.float32)).astype(jnp.bfloat16)
    return high, low


def three_pass(left, right, left_dim, right_dim):
    dims = (((left_dim,), (right_dim,)), ((), ()))
    f32 = jnp.float32
    rows = left[0].shape[0]
    stacked = jnp.concatenate(left, axis=0)
    main = lax.dot_general(stacked, right[0], dims, preferred_element_type=f32)
    side = lax.dot_general(left[0], right[1], dims, preferred_element_type=f32)
    return main[:rows] + (main[rows:] + side)


def act_kernel(cols_ref, rows_ref, g_ref, c_ref, local_ref, back_ref, ahead_ref, acc):
    count, nbrs, tile, _ = g_ref.shape
    rows = rows_ref.shape[0]
    acc[...] = jnp.zeros_like(acc)

    def step(t, carry):
        left = split(rows_ref[:, pl.ds(pl.multiple_of(t * tile, tile), tile)])
        for i, ref in enumerate((g_ref, c_ref)):
            for k in range(nbrs):
                part = three_pass(left, split(ref[t, k]), 1, 0)
                at = cols_ref[t, k]
                acc[at, i * rows : (i + 1) * rows, :] += part
        return carry

    lax.fori_loop(0, count, step, 0)
    for t in range(count):
        local_ref[:, t * tile : (t + 1) * tile] = acc[t]
    back_ref[...] = acc[count]
    ahead_ref[...] = acc[count + 1]


def transposed_action(tile_cols, rows, g_tiles, c_tiles):
    count, nbrs, tile, _ = g_tiles.shape
    num, nodes = rows.shape
    vmem = pl.BlockSpec(memory_space=pltpu.VMEM)
    f32 = jnp.float32
    return pl.pallas_call(
        act_kernel,
        out_shape=(
            jax.ShapeDtypeStruct((2 * num, nodes), f32),
            jax.ShapeDtypeStruct((2 * num, tile), f32),
            jax.ShapeDtypeStruct((2 * num, tile), f32),
        ),
        in_specs=[pl.BlockSpec(memory_space=pltpu.SMEM), vmem, vmem, vmem],
        out_specs=(vmem,) * 3,
        scratch_shapes=[pltpu.VMEM((count + 2, 2 * num, tile), f32)],
        name="transposed_action",
    )(tile_cols, rows, g_tiles, c_tiles)


def work_kernel(cols_ref, block_ref, before_ref, after_ref, c_ref, dinv_ref, out_ref, ext):
    count, nbrs, tile, _ = c_ref.shape
    for t in range(count):
        ext[t] = block_ref[:, t * tile : (t + 1) * tile]
    ext[count] = before_ref[...]
    ext[count + 1] = after_ref[...]
    for t in range(count):
        total = 0.0
        for k in range(nbrs):
            left = split(ext[cols_ref[t, k]])
            total = total + three_pass(left, split(c_ref[t, k]), 1, 1)
        lanes = slice(t * tile, (t + 1) * tile)
        out_ref[:, lanes] = dinv_ref[:, lanes] * total


def scaled_action(tile_cols, block, before, after, c_tiles, dinv):
    count, nbrs, tile, _ = c_tiles.shape
    vmem = pl.BlockSpec(memory_space=pltpu.VMEM)
    return pl.pallas_call(
        work_kernel,
        out_shape=jax.ShapeDtypeStruct(block.shape, jnp.float32),
        in_specs=[pl.BlockSpec(memory_space=pltpu.SMEM)] + [vmem] * 5,
        out_specs=vmem,
        scratch_shapes=[pltpu.VMEM((count + 2, block.shape[0], tile), jnp.float32)],
        name="scaled_action",
    )(tile_cols, block, before, after, c_tiles, dinv[None, :])


def first_kernel(work_ref, *refs):
    pieces, (coeff_ref, high_ref, low_ref) = refs[:-3], refs[-3:]
    left = split(work_ref[...])
    at = 0
    for ref in pieces:
        rows = ref.shape[0]
        right = split(ref[...])
        high_ref[at : at + rows, :] = right[0]
        low_ref[at : at + rows, :] = right[1]
        coeff_ref[:, at : at + rows] = three_pass(left, right, 1, 1)
        at += rows


def first_coefficients(work, pieces):
    rows = sum(p.shape[0] for p in pieces)
    vmem = pl.BlockSpec(memory_space=pltpu.VMEM)
    bf16 = jnp.bfloat16
    return pl.pallas_call(
        first_kernel,
        out_shape=(
            jax.ShapeDtypeStruct((work.shape[0], rows), jnp.float32),
            jax.ShapeDtypeStruct((rows, work.shape[1]), bf16),
            jax.ShapeDtypeStruct((rows, work.shape[1]), bf16),
        ),
        in_specs=[vmem] * (1 + len(pieces)),
        out_specs=(vmem,) * 3,
        name="first_coefficients",
    )(work, *pieces)


def product_kernel(right_dim, left_ref, *refs):
    rows, out_ref = refs[:-1], refs[-1]
    at, total = 0, 0.0
    for high_ref, low_ref in zip(rows[::2], rows[1::2]):
        right = (high_ref[...], low_ref[...])
        count = high_ref.shape[0]
        if right_dim == 1:
            left = split(left_ref[...])
            out_ref[:, at : at + count] = three_pass(left, right, 1, 1)
        else:
            left = split(left_ref[:, at : at + count])
            total = total + three_pass(left, right, 1, 0)
        at += count
    if right_dim == 0:
        out_ref[...] = total


def wide_product(left, rows, right_dim):
    vmem = pl.BlockSpec(memory_space=pltpu.VMEM)
    cols = rows[0].shape[1]
    if right_dim == 1:
        cols = sum(r.shape[0] for r in rows[::2])
    return pl.pallas_call(
        functools.partial(product_kernel, right_dim),
        out_shape=jax.ShapeDtypeStruct((left.shape[0], cols), jnp.float32),
        in_specs=[vmem] * (1 + len(rows)),
        out_specs=vmem,
        name="wide_product",
    )(left, *rows)


def pair_kernel(
    core_ref, same_ref, across_ref, basis_ref, second_ref, local_ref, back_ref,
    ahead_ref, edge_ref, out_ref, all_ref
):
    core = core_ref[0]
    nx, own, nodes = same_ref.shape
    for i in range(nx):
        all_ref[2 * i + core] = same_ref[i]
        all_ref[2 * i + 1 - core] = across_ref[i]
    ports = 2 * nx * own
    left = split(all_ref[...].reshape(ports, nodes))
    rim = split(back_ref[...] + ahead_ref[...])
    hot = edge_ref[...].astype(jnp.bfloat16)
    dims = (((1,), (0,)), ((), ()))
    f32 = jnp.float32
    image = local_ref[...] + (
        lax.dot_general(rim[0], hot, dims, preferred_element_type=f32)
        + lax.dot_general(rim[1], hot, dims, preferred_element_type=f32)
    )
    wide = basis_ref.shape[0]
    out_ref[:, :wide] = three_pass(left, split(basis_ref[...]), 1, 1)
    tail = jnp.concatenate([second_ref[...], image], axis=0)
    out_ref[:, wide:] = three_pass(left, split(tail), 1, 1)


def pair_products(core, same, across, basis_images, second, local, back, ahead, edge_hot):
    nx, own, nodes = same.shape
    ports = 2 * nx * own
    vmem = pl.BlockSpec(memory_space=pltpu.VMEM)
    f32 = jnp.float32
    lanes = basis_images.shape[0] + 3 * own
    out, all_rows = pl.pallas_call(
        pair_kernel,
        out_shape=(
            jax.ShapeDtypeStruct((ports, lanes), f32),
            jax.ShapeDtypeStruct((2 * nx, own, nodes), f32),
        ),
        in_specs=[pl.BlockSpec(memory_space=pltpu.SMEM)] + [vmem] * 8,
        out_specs=(vmem,) * 2,
        name="pair_products",
    )(core[None].astype(jnp.int32), same, across, basis_images, second, local, back, ahead, edge_hot)
    return out, all_rows.reshape(ports, nodes)


EDGE = 64


def factor_kernel(own, col_ref, gram_ref, second_ref, new_ref, chol_ref, inverse, work, factor):
    ports = gram_ref.shape[0]
    gram = gram_ref[...]
    work[...] = 0.5 * (gram + gram.T)
    factor[...] = jnp.zeros_like(factor)
    inverse[...] = jnp.zeros_like(inverse)
    row_ids = lax.broadcasted_iota(jnp.int32, (EDGE, 2 * EDGE), 0)
    lane_ids = lax.broadcasted_iota(jnp.int32, (EDGE, 2 * EDGE), 1)
    eye = (lane_ids - EDGE == row_ids).astype(jnp.float32)
    for k in range(ports // EDGE):
        lo, hi = k * EDGE, (k + 1) * EDGE
        pair = jnp.concatenate([work[lo:hi, lo:hi], eye[:, EDGE:]], axis=1)
        for j in range(EDGE - 1):
            group = j // 8 * 8
            pivot = pair[j : j + 1, :]
            pivot = pivot * (1.0 / pivot[:, j : j + 1])
            column = pair[group : group + 8, j : j + 1]
            column = jnp.where(row_ids[group : group + 8, :1] > j, column, 0.0)
            parts = [pair[group : group + 8] - column * pivot]
            if group > 0:
                parts.insert(0, pair[:group])
            if group + 8 < EDGE:
                rest = pair[group + 8 :]
                parts.append(rest - rest[:, j : j + 1] * pivot)
            pair = jnp.concatenate(parts, axis=0)
        diag = jnp.sum(
            jnp.where(lane_ids == row_ids, pair, 0.0), axis=1, keepdims=True
        )
        pair = pair * lax.rsqrt(diag)
        upper = jnp.where(
            lane_ids[:, :EDGE] >= row_ids[:, :EDGE], pair[:, :EDGE], 0.0
        )
        small = pair[:, EDGE:]
        factor[lo:hi, lo:hi] = upper.T
        if hi < ports:
            panel = exact(work[hi:, lo:hi], small, 1, 1)
            factor[hi:, lo:hi] = panel
            work[hi:, hi:] = work[hi:, hi:] - exact(panel, panel, 1, 1)
        start = (
            lax.broadcasted_iota(jnp.int32, (EDGE, ports), 1)
            == lax.broadcasted_iota(jnp.int32, (EDGE, ports), 0) + lo
        ).astype(jnp.float32)
        if k > 0:
            start = start - exact(factor[lo:hi, :lo], inverse[:lo, :], 1, 0)
        inverse[lo:hi, :] = exact(small, start, 1, 0)
    rows = pl.ds(pl.multiple_of(col_ref[0] * own, own), own)
    chol_ref[...] = factor[rows, :]
    new_ref[...] = exact(inverse[rows, :], second_ref[...], 1, 0)


def factor_block(col, gram, second_all, own):
    ports, nodes = second_all.shape
    f32 = jnp.float32
    vmem = pl.BlockSpec(memory_space=pltpu.VMEM)
    return pl.pallas_call(
        functools.partial(factor_kernel, own),
        out_shape=(
            jax.ShapeDtypeStruct((own, nodes), f32),
            jax.ShapeDtypeStruct((own, ports), f32),
            jax.ShapeDtypeStruct((ports, ports), f32),
        ),
        in_specs=[pl.BlockSpec(memory_space=pltpu.SMEM), vmem, vmem],
        out_specs=(vmem,) * 3,
        scratch_shapes=[pltpu.VMEM((ports, ports), f32)] * 2,
        cost_estimate=pl.CostEstimate(
            flops=20_000_000_000, transcendentals=0, bytes_accessed=2_000_000
        ),
        name="factor_block",
    )(col, gram, second_all)


def finish_kernel(own, brows, col_ref, full_ref, inverse_ref, *outs):
    g_proj_ref, c_proj_ref, g_new_ref, c_new_ref = outs
    ports = full_ref.shape[0]
    rows = pl.ds(pl.multiple_of(col_ref[0] * own, own), own)
    inverse = inverse_ref[...]
    inverse_own = inverse_ref[rows, :]
    g_proj_ref[...] = exact(full_ref[:, :brows].T, inverse, 1, 1)
    c_proj_ref[...] = exact(full_ref[:, brows : 2 * brows].T, inverse, 1, 1)
    for i, out_ref in enumerate((g_new_ref, c_new_ref)):
        at = 2 * brows + i * ports
        core = full_ref[:, at : at + ports]
        out_ref[...] = exact(exact(inverse_own, core, 1, 1), inverse, 1, 1)


def finish_block(col, full, inverse, own, brows):
    ports = inverse.shape[0]
    f32 = jnp.float32
    vmem = pl.BlockSpec(memory_space=pltpu.VMEM)
    return pl.pallas_call(
        functools.partial(finish_kernel, own, brows),
        out_shape=(
            jax.ShapeDtypeStruct((brows, ports), f32),
            jax.ShapeDtypeStruct((brows, ports), f32),
            jax.ShapeDtypeStruct((own, ports), f32),
            jax.ShapeDtypeStruct((own, ports), f32),
        ),
        in_specs=[pl.BlockSpec(memory_space=pltpu.SMEM), vmem, vmem],
        out_specs=(vmem,) * 4,
        name="finish_block",
    )(col, full, inverse)


def on_device(block, basis, g_tiles, c_tiles, tile_cols, bnd_rows, dinv, port_nodes):
    tile = g_tiles.shape[-1]
    nodes = block.shape[1]
    own = block.shape[0]
    brows = basis.shape[0]
    width = nodes // tile + 2
    nx = lax.axis_size("x")
    xi = lax.axis_index("x")
    core = lax.axis_index("core")
    dom = lax.axis_index(DOM)
    col = xi * 2 + core
    half = brows // 2

    right = shift(basis, "x", -1)
    left = shift(basis, "x", 1)
    far_low = shift(left[:half], "x", 1)
    far_high = shift(right[half:], "x", -1)

    node_ids = jnp.arange(nodes, dtype=jnp.int32)
    edge_hot = (bnd_rows[:, None] == node_ids[None, :]).astype(jnp.float32)
    port_hot = ((port_nodes - dom * nodes)[:, None] == node_ids[None, :]).astype(
        jnp.float32
    )

    rim = contract(block, edge_hot, 1, 1)
    before = shift_open(rim, DOM, 1)
    after = shift_open(rim, DOM, -1)
    work = scaled_action(tile_cols, block, before, after, c_tiles, dinv)
    other = shift(work, "core", 1)
    low = jnp.where(core == 0, work, other)
    high = jnp.where(core == 0, other, work)
    work_chip = jnp.concatenate([low, high], axis=0)

    def exchange(back, ahead):
        return shift_open(back, DOM, -1), shift_open(ahead, DOM, 1)

    port_part = exact(port_hot, basis, 1, 1)
    work_chip, port_part = lax.optimization_barrier((work_chip, port_part))

    near, near_high, near_low = first_coefficients(work_chip, (basis, right, left))
    last, far_high, far_low = first_coefficients(work_chip, (far_low, far_high))
    partial = jnp.concatenate([near, last], axis=1)
    rows_split = (near_high, near_low, far_high, far_low)

    partial, basis_rows = lax.optimization_barrier((partial, basis))
    basis_local, basis_back, basis_ahead = transposed_action(
        tile_cols, basis_rows, g_tiles, c_tiles
    )
    first_coeff, port_sum = sum_dom(partial, port_part)
    first_coeff, basis_local, basis_back, basis_ahead = lax.optimization_barrier(
        (first_coeff, basis_local, basis_back, basis_ahead)
    )
    basis_rims = exchange(basis_back, basis_ahead)
    port_proj = port_sum.T
    drop = wide_product(first_coeff, rows_split, 0)
    first_chip = work_chip - (drop + shift(drop, "core", 1))
    (second_coeff,), basis_rims = sum_dom(
        wide_product(first_chip, rows_split, 1), beside=basis_rims
    )
    basis_images = basis_local + contract(sum(basis_rims), edge_hot, 1, 0)
    drop = wide_product(second_coeff, rows_split, 0)
    drop_low, drop_high = drop[:own], drop[own:]
    mine = jnp.where(core == 0, drop_low, drop_high)
    theirs = jnp.where(core == 0, drop_high, drop_low)
    first_own = jnp.where(core == 0, first_chip[:own], first_chip[own:])
    second = first_own - (mine + shift(theirs, "core", 1))
    second, basis_images = lax.optimization_barrier((second, basis_images))

    local, back, ahead = transposed_action(tile_cols, second, g_tiles, c_tiles)
    back, ahead = exchange(back, ahead)

    same = spread(second, "x")
    same, back, ahead = lax.optimization_barrier((same, back, ahead))
    across = shift(same, "core", 1)
    products, second_all = pair_products(
        core, same, across, basis_images, second, local, back, ahead, edge_hot
    )
    products, coeff_sum = lax.optimization_barrier(
        (products, first_coeff + second_coeff)
    )
    piece = sum_rows_to_piece(products)

    slots = coeff_sum.reshape(2 * own, nx, brows)
    order = (0, 1, 3, 2)
    landed = [slots[:, 0]]
    landed += [shift(slots[:, order[k]], "x", k) for k in range(1, nx)]
    landed = jnp.roll(jnp.stack(landed[::-1]), xi + 1, axis=0)
    coeffs = landed.reshape(nx * 2 * own, brows).T

    ports_piece = piece.shape[0]
    ports = 2 * nx * own
    narrow = spread(piece[:, 2 * brows :], ("x", "core"))
    narrow = narrow.reshape(2 * nx, ports_piece, 3, own).transpose(1, 2, 0, 3)
    narrow = narrow.reshape(ports_piece, 3 * ports)
    gram = piece_to_rows(narrow[:, :ports])
    rest = jnp.concatenate([piece[:, : 2 * brows], narrow[:, ports:]], axis=1)
    gram, rest = lax.optimization_barrier((gram, rest))
    full = piece_to_rows(rest)
    where = col[None].astype(jnp.int32)
    new_block, chol_rows, inverse = factor_block(where, gram, second_all, own)
    g_proj, c_proj, g_new, c_new = finish_block(where, full, inverse, own, brows)
    return (new_block, coeffs, chol_rows, port_proj, g_proj, c_proj, g_new, c_new)


def solution(mesh):
    sizes = (8, 8, 4, 2) if mesh.devices.size == 512 else (2, 2, 4, 2)
    fine = Mesh(mesh.devices.reshape(sizes), ("z", "y", "x", "core"))
    dom, col = ("z", "y"), ("x", "core")
    placed = (
        P(col, dom),
        P(col, dom),
        P(dom, None, None, None),
        P(dom, None, None, None),
        P(dom, None),
        P(dom),
        P(dom),
        P(),
    )
    return jax.shard_map(
        on_device,
        mesh=fine,
        in_specs=placed,
        out_specs=(P(col, dom),) + (P(col, None),) * 7,
        check_vma=False,
    )
```
